256 devices in a mesh: chain: 8 (over x, y_lo), tok: 32 (over y_hi, z, core).
Axes of the slice: x: 4, y: 4 (y_hi: 2, y_lo: 2; y = y_hi * 2 + y_lo), z: 8, core: 2. Of those that a mesh axis runs over, the one named last changes fastest.
Arguments:
- layer_activations: bfloat16 [8192, 8192], P('tok'), may hold values from -6 to 6
- rotated_probes: bfloat16 [8192, 8192], P('tok'), may hold values from -6 to 6
- attended_contents: bfloat16 [8192, 1024], P('tok'), may hold values from -6 to 6
- attended_slope: bfloat16 [8192, 8192], P('tok'), may hold values from -6 to 6
- locked_projection: bfloat16 [8192, 1024], P('tok', 'chain'), may hold values from -0.044194174 to 0.044194174
- first_multipliers: float32 [16, 8192, 64], P('chain', 'tok'), may hold values from -6 to 6
- second_multipliers: float32 [16, 64, 1024], P('chain', None, 'tok'), may hold values from -6 to 6
- first_jitter: float32 [16, 8192, 64], P('chain', 'tok'), may hold values from -6 to 6
- second_jitter: float32 [16, 64, 1024], P('chain', None, 'tok'), may hold values from -6 to 6
- chain_heats: float32 [16], P('chain'), may hold values from 0.05 to 1
- donor_chain: int32 [16], replicated, may hold values from 0 to 15, each once
Outputs:
- new_a: float32 [16, 8192, 64], P('chain', 'tok')
- new_b: float32 [16, 64, 1024], P('chain', None, 'tok')
The draws below stay inside these ranges and needn't reach their ends.
All inputs are finite; a program needn't handle non-finite values.
Results may differ from the reference program's by a relative error of at most 0.019.
Values may be sent and summed in bfloat16 or wider, within the bound.
A program may use at most 128 MiB of HBM per device.

```python
import math
import jax
import jax.numpy as jnp
from jax import lax

MODEL_WIDTH = 8192
QUERY_HEADS = 64
KEY_HEADS = 8
HEAD_SIZE = 128
ADAPTER_RANK = 64
SEQUENCE_TOKENS = 256
KEY_WIDTH = 1024
CHAIN_NUMBER = 16
TOKEN_TOTAL = 8192


def draw_weight_matrix(key):
    weight_key = jax.random.fold_in(key, 101)
    return jax.random.truncated_normal(weight_key, -4.0, 4.0, (MODEL_WIDTH, KEY_WIDTH), jnp.float32) * (1.0 / math.sqrt(MODEL_WIDTH))


def hot_layout(key):
    sequence_count = TOKEN_TOTAL // SEQUENCE_TOKENS
    query_group = QUERY_HEADS // KEY_HEADS
    weight = draw_weight_matrix(key)
    weight_low = weight.astype(jnp.bfloat16).astype(jnp.float32)
    seq_ids = jnp.arange(sequence_count, dtype=jnp.int32)
    is_hot = seq_ids % 3 == 0
    level = 3.0 + 1.5 * (seq_ids // 3 % 3).astype(jnp.float32)
    row_noise = jax.random.normal(jax.random.fold_in(key, 102), (sequence_count, MODEL_WIDTH), jnp.float32)
    first_row = (level[:, None] * jnp.tanh(2.0 * row_noise)).astype(jnp.bfloat16).astype(jnp.float32)
    drawn_rows = jnp.dot(first_row, weight_low, precision=lax.Precision.HIGHEST)
    per_head_keys = drawn_rows.reshape(sequence_count, KEY_HEADS, 1, HEAD_SIZE)
    head_factor = jax.random.uniform(jax.random.fold_in(key, 103), (sequence_count, KEY_HEADS, query_group, 1), jnp.float32, 0.6, 1.0)
    hot_query = 6.0 * head_factor * jnp.tanh(2.0 * per_head_keys / level[:, None, None, None])
    score_top = jnp.max(jnp.sum(hot_query * per_head_keys, axis=-1), axis=(1, 2)) / math.sqrt(HEAD_SIZE)
    shrink = 1.0 - 2.0 / jnp.maximum(score_top, 4.0)
    second_row = shrink[:, None] * first_row
    return (is_hot, first_row, second_row, hot_query.reshape(sequence_count, QUERY_HEADS * HEAD_SIZE))


def draw_locked_projection(key, part):
    return draw_weight_matrix(key).astype(jnp.bfloat16)


def draw_layer_activations(key, part):
    sequence_count = TOKEN_TOTAL // SEQUENCE_TOKENS
    is_hot, first_row, second_row, hot_query = hot_layout(key)
    drawn = jax.random.truncated_normal(jax.random.fold_in(key, 104), -6.0, 6.0, (sequence_count, SEQUENCE_TOKENS, MODEL_WIDTH), jnp.float32)
    position = jnp.arange(SEQUENCE_TOKENS, dtype=jnp.int32)[None, :, None]
    hot = is_hot[:, None, None]
    drawn = jnp.where(hot & (position == SEQUENCE_TOKENS - 4), first_row[:, None, :], drawn)
    drawn = jnp.where(hot & (position == SEQUENCE_TOKENS - 3), second_row[:, None, :], drawn)
    return drawn.reshape(TOKEN_TOTAL, MODEL_WIDTH).astype(jnp.bfloat16)


def draw_rotated_probes(key, part):
    sequence_count = TOKEN_TOTAL // SEQUENCE_TOKENS
    is_hot, first_row, second_row, hot_query = hot_layout(key)
    drawn = jax.random.truncated_normal(jax.random.fold_in(key, 105), -6.0, 6.0, (sequence_count, SEQUENCE_TOKENS, QUERY_HEADS * HEAD_SIZE), jnp.float32)
    position = jnp.arange(SEQUENCE_TOKENS, dtype=jnp.int32)[None, :, None]
    hot = is_hot[:, None, None]
    drawn = jnp.where(hot & (position == SEQUENCE_TOKENS - 2), hot_query[:, None, :], drawn)
    drawn = jnp.where(hot & (position == SEQUENCE_TOKENS - 1), 0.8 * hot_query[:, None, :], drawn)
    return drawn.reshape(TOKEN_TOTAL, QUERY_HEADS * HEAD_SIZE).astype(jnp.bfloat16)


def level_of(rng, dims, cuts, smallest, largest):
    factor_of, own = 1.0, jax.random.fold_in(rng, 6)
    for dim, blocks in cuts:
        draws = jnp.exp(jax.random.uniform(jax.random.fold_in(own, dim), (blocks,), jnp.float32, smallest / len(cuts), largest / len(cuts)))
        factor_of = factor_of * jnp.repeat(draws, dims[dim] // blocks).reshape([-1 if axis == dim else 1 for axis in range(len(dims))])
    return factor_of


def gaussian(rng, extent, width, reach, split=(), kind=jnp.bfloat16):
    drawn = jax.random.normal(rng, extent, jnp.float32) * width
    if len(split) > 0:
        drawn = level_of(rng, extent, split, -0.22, 0.18) * drawn
    return jnp.clip(drawn, min=-reach, max=reach).astype(kind)


def setup_inputs(seed: int = 0) -> dict:
    arg_keys = jax.random.split(jax.random.key(seed), 12)
    return {
        "layer_activations": draw_layer_activations(jax.random.fold_in(arg_keys[11], 71), 0),
        "rotated_probes": draw_rotated_probes(jax.random.fold_in(arg_keys[11], 71), 0),
        "attended_contents": gaussian(arg_keys[2], (TOKEN_TOTAL, KEY_WIDTH), 1.0, 6.0, ((0, 32),)),
        "attended_slope": gaussian(arg_keys[3], (TOKEN_TOTAL, QUERY_HEADS * HEAD_SIZE), 1.0, 6.0, ((0, 32),)),
        "locked_projection": draw_locked_projection(jax.random.fold_in(arg_keys[11], 71), 0),
        "first_multipliers": gaussian(arg_keys[5], (CHAIN_NUMBER, MODEL_WIDTH, ADAPTER_RANK), 1.0, 6.0, ((0, 8), (1, 32)), jnp.float32),
        "second_multipliers": gaussian(arg_keys[6], (CHAIN_NUMBER, ADAPTER_RANK, KEY_WIDTH), 1.0, 6.0, ((0, 8), (2, 32)), jnp.float32),
        "first_jitter": gaussian(arg_keys[7], (CHAIN_NUMBER, MODEL_WIDTH, ADAPTER_RANK), 1.0, 6.0, ((0, 8), (1, 32)), jnp.float32),
        "second_jitter": gaussian(arg_keys[8], (CHAIN_NUMBER, ADAPTER_RANK, KEY_WIDTH), 1.0, 6.0, ((0, 8), (2, 32)), jnp.float32),
        "chain_heats": jnp.clip(jnp.exp(math.log(1.0) - 2.9957323 * jax.random.uniform(arg_keys[9], (CHAIN_NUMBER,), jnp.float32) ** level_of(arg_keys[9], (CHAIN_NUMBER,), ((0, 8),), -0.2, 0.2)), 0.05, 1.0),
        "donor_chain": jax.random.permutation(arg_keys[10], CHAIN_NUMBER).astype(jnp.int32),
    }


STRIDE_LENGTH = 0.2

def key_gradient(query_item, key_item, value_item, grad_item):
    score_scale = 1.0 / math.sqrt(HEAD_SIZE)
    query_f = query_item.astype(jnp.float32)
    scores = jnp.einsum('tjd,sd->jts', query_f, key_item.astype(jnp.float32)) * score_scale
    length = key_item.shape[0]
    future_mask = lax.broadcasted_iota(jnp.int32, (length, length), 1) > lax.broadcasted_iota(jnp.int32, (length, length), 0)
    scores = jnp.where(future_mask[None], -1e+30, scores)
    row_max = lax.optimization_barrier(jnp.max(scores, axis=-1, keepdims=True))
    expo = jnp.exp(scores - row_max)
    attn_weights = expo / lax.optimization_barrier(jnp.sum(expo, axis=-1, keepdims=True))
    dweights = jnp.einsum('tjd,sd->jts', grad_item.astype(jnp.float32), value_item.astype(jnp.float32))
    center = lax.optimization_barrier(jnp.sum(attn_weights * dweights, axis=-1, keepdims=True))
    dscores = (attn_weights * (dweights - center)).astype(jnp.bfloat16)
    return jnp.einsum('jts,tjd->sd', dscores.astype(jnp.float32), query_f) * score_scale

def head_items(numeric_array, sequence_count, query_group):
    return numeric_array.reshape(sequence_count, SEQUENCE_TOKENS, KEY_HEADS, query_group, HEAD_SIZE).transpose(0, 2, 1, 3, 4).reshape(sequence_count * KEY_HEADS, SEQUENCE_TOKENS, query_group, HEAD_SIZE)

def key_items(numeric_array, sequence_count):
    return numeric_array.reshape(sequence_count, SEQUENCE_TOKENS, KEY_HEADS, HEAD_SIZE).transpose(0, 2, 1, 3).reshape(sequence_count * KEY_HEADS, SEQUENCE_TOKENS, HEAD_SIZE)

def reference(layer_activations, rotated_probes, attended_contents, attended_slope, locked_projection, first_multipliers, second_multipliers, first_jitter, second_jitter, chain_heats, donor_chain):
    adapter_scale = 1.0 / math.sqrt(MODEL_WIDTH * ADAPTER_RANK)
    sequence_count = TOKEN_TOTAL // SEQUENCE_TOKENS
    query_group = QUERY_HEADS // KEY_HEADS
    query_tensor = head_items(rotated_probes, sequence_count, query_group)
    gradient_total = head_items(attended_slope, sequence_count, query_group)
    value_tensor = key_items(attended_contents, sequence_count)
    plain_keys = jnp.dot(layer_activations, locked_projection, preferred_element_type=jnp.float32).astype(jnp.bfloat16)
    contract_product = (((0,), (0,)), ((), ()))

    def one_chain(chain_ordinal):
        a_low = first_multipliers[chain_ordinal].astype(jnp.bfloat16)
        right_low_rank = second_multipliers[chain_ordinal].astype(jnp.bfloat16)
        low_rank_keys = jnp.dot(layer_activations, a_low, preferred_element_type=jnp.float32).astype(jnp.bfloat16)
        key_rows = (plain_keys.astype(jnp.float32) + adapter_scale * jnp.dot(low_rank_keys, right_low_rank, preferred_element_type=jnp.float32)).astype(jnp.bfloat16)
        key_tensor = key_items(key_rows, sequence_count)
        step_result = lax.map(lambda items: key_gradient(*items), (query_tensor, key_tensor, value_tensor, gradient_total))
        key_input_gradient = step_result.reshape(sequence_count, KEY_HEADS, SEQUENCE_TOKENS, HEAD_SIZE).transpose(0, 2, 1, 3).reshape(TOKEN_TOTAL, KEY_WIDTH).astype(jnp.bfloat16)
        low_rank_gradient = (adapter_scale * jnp.dot(key_input_gradient, right_low_rank.T, preferred_element_type=jnp.float32)).astype(jnp.bfloat16)
        first_slope = lax.dot_general(layer_activations, low_rank_gradient, contract_product, preferred_element_type=jnp.float32)
        second_slope = adapter_scale * lax.dot_general(low_rank_keys, key_input_gradient, contract_product, preferred_element_type=jnp.float32)
        chain_heat = jnp.sqrt(2.0 * STRIDE_LENGTH * chain_heats[chain_ordinal])
        shifted_first = first_multipliers[chain_ordinal] - STRIDE_LENGTH * (first_slope + first_multipliers[chain_ordinal]) + chain_heat * first_jitter[chain_ordinal]
        shifted_second = second_multipliers[chain_ordinal] - STRIDE_LENGTH * (second_slope + second_multipliers[chain_ordinal]) + chain_heat * second_jitter[chain_ordinal]
        return (shifted_first, shifted_second)
    shifted_first, shifted_second = lax.map(one_chain, jnp.arange(CHAIN_NUMBER, dtype=jnp.int32))
    return (shifted_first[donor_chain], shifted_second[donor_chain])
```

```python
import functools
import math

import jax
import jax.numpy as jnp
from jax import lax
from jax.experimental import pallas as pl
from jax.experimental.pallas import tpu as pltpu
from jax.sharding import PartitionSpec as P

MESH = pl.DeviceIdType.MESH
HEAD = 128
RANK = 64
MODEL_WIDTH = 8192
STRIDE_LENGTH = 0.2
ADAPTER_SCALE = 1.0 / math.sqrt(MODEL_WIDTH * RANK)
SCORE_SCALE = 1.0 / math.sqrt(HEAD)
EXP2_SCALE = SCORE_SCALE * math.log2(math.e)
VMEM_LIMIT = 56 * 1024 * 1024

F32 = jnp.float32
BF16 = jnp.bfloat16


def dot(a, b, dims=((1,), (0,))):
    return lax.dot_general(a, b, (dims, ((), ())), preferred_element_type=F32)


class Place:
    def __init__(self, nc, nt):
        self.nc, self.nt, self.nz = nc, nt, nt // 4
        self.c = lax.axis_index("chain")
        self.t = lax.axis_index("tok")
        self.k = lax.rem(self.t, 2)
        self.z = lax.rem(self.t // 2, self.nz)
        self.yh = self.t // (2 * self.nz)

    def tok(self, other_yh, dz, other_k=False):
        yh = 1 - self.yh if other_yh else self.yh
        k = 1 - self.k if other_k else self.k
        z = lax.rem(self.z + (dz + self.nz), self.nz)
        return (yh * self.nz + z) * 2 + k

    def chain(self, i):
        return lax.rem(self.c + i, self.nc)


def entry_barrier(devices, extra=()):
    barrier = pltpu.get_barrier_semaphore()
    for dev in devices:
        pl.semaphore_signal(barrier, inc=1, device_id=dev, device_id_type=MESH)
    count = len(devices)
    for dev, present in extra:

        @pl.when(present)
        def _():
            pl.semaphore_signal(barrier, inc=1, device_id=dev, device_id_type=MESH)

        count = count + present.astype(jnp.int32)
    pl.semaphore_wait(barrier, count)


def gather_kernel(nc, nt, wab_ref, x_ref, base_ref, lr_ref, bt_ref, full, bts, acc, ssem, rsem, csem, lsem):
    at = Place(nc, nt)
    nz, half = at.nz, at.nz // 2
    rb = x_ref.shape[1] // nt
    cb = (wab_ref.shape[0] - rb) * 2
    left, right = (at.c, at.tok(0, -1)), (at.c, at.tok(0, 1))
    across, sibling = (at.c, at.tok(1, 0)), (at.c, at.tok(0, 0, True))
    peers = [(at.chain(i), at.t) for i in range(1, nc)]
    entry_barrier([left, right, across, sibling] + peers)
    sends = []

    def send(b, dev, own=False):
        cp = pltpu.make_async_remote_copy(
            src_ref=wab_ref if own else full.at[b],
            dst_ref=full.at[b],
            send_sem=ssem.at[len(sends)],
            recv_sem=rsem.at[b],
            device_id=dev,
            device_id_type=MESH,
        )
        cp.start()
        sends.append(cp)

    def wait(b):
        pltpu.make_async_remote_copy(
            src_ref=full.at[b],
            dst_ref=full.at[b],
            send_sem=ssem.at[0],
            recv_sem=rsem.at[b],
            device_id=sibling,
            device_id_type=MESH,
        ).wait_recv()

    me = at.t
    send(me, across, True)
    send(me, right, True)
    send(me, left, True)
    send(me, sibling, True)
    own = pltpu.make_async_copy(wab_ref, full.at[me], lsem.at[0])
    own.start()

    def arrive(other_yh, dz, onward):
        b = at.tok(other_yh, dz)
        wait(b)
        for dev in onward:
            send(b, dev)
        send(b, sibling)

    events = []
    for s in range(1, half + 1):
        events.append((2 * s, 0, -s, right if s < half else None))
        if s <= half - 1:
            events.append((2 * s, 0, s, left if s < half - 1 else None))
            events.append((2 * s + 1.5, 1, -s, right if s < half - 1 else None))
        events.append((2 * s + 1.5, 1, s, left if s < half else None))
    events.sort(key=lambda e: e[0])
    crossed = False
    for when, other_yh, dz, onward in events:
        if not crossed and when > 2:
            arrive(1, 0, [right, left])
            crossed = True
        arrive(other_yh, dz, [onward] if onward is not None else [])
    own.wait()
    for dz in range(nz):
        for other_yh in (0, 1):
            wait(at.tok(other_yh, dz, True))

    hb = cb // 2
    for b in range(nt):
        bts[pl.ds(b * cb, hb), :] = full[b, pl.ds(rb, hb), pl.ds(0, HEAD)]
        bts[pl.ds(b * cb + hb, hb), :] = full[b, pl.ds(rb, hb), pl.ds(HEAD, HEAD)]
    exchanges = []

    def exchange(src, dst, i, kind):
        cp = pltpu.make_async_remote_copy(
            src_ref=src,
            dst_ref=dst.at[at.c],
            send_sem=csem.at[kind, 0, i],
            recv_sem=csem.at[kind, 1, i],
            device_id=(at.chain(i), at.t),
            device_id_type=MESH,
        )
        cp.start()
        exchanges.append(cp)

    for i in range(1, nc):
        exchange(bts.at[pl.ds(pl.multiple_of(at.chain(i) * HEAD, HEAD), HEAD)], bt_ref, i, 0)
    bt_ref[at.c] = bts[pl.ds(pl.multiple_of(at.c * HEAD, HEAD), HEAD), :]

    acc[...] = jnp.zeros_like(acc)

    def step(b, carry):
        cols = pl.ds(pl.multiple_of(b * rb, rb), rb)
        acc[...] += dot(x_ref[:, cols], full[b, pl.ds(0, rb), :])
        return carry

    lax.fori_loop(0, nt, step, 0)
    lr_ref[at.c] = acc[:, HEAD:].astype(BF16)
    for i in range(1, nc):
        exchange(lr_ref.at[at.c], lr_ref, i, 1)
    base_ref[...] = acc[:, :HEAD].astype(BF16)
    for cp in exchanges:
        cp.wait()
    for cp in sends:
        cp.wait_send()


def gather_and_project(nc, nt, wab, x):
    tokens = x.shape[0]
    rows = wab.shape[0]
    vmem = pl.BlockSpec(memory_space=pltpu.VMEM)
    return pl.pallas_call(
        functools.partial(gather_kernel, nc, nt),
        out_shape=(
            jax.ShapeDtypeStruct((tokens, HEAD), BF16),
            jax.ShapeDtypeStruct((nc, tokens, HEAD), BF16),
            jax.ShapeDtypeStruct((nc, HEAD, HEAD), BF16),
        ),
        in_specs=[vmem] * 2,
        out_specs=(vmem,) * 3,
        scratch_shapes=[
            pltpu.VMEM((nt, rows, 2 * HEAD), BF16),
            pltpu.VMEM((nc * HEAD, HEAD), BF16),
            pltpu.VMEM((tokens, 2 * HEAD), F32),
            pltpu.SemaphoreType.DMA((2 * nt,)),
            pltpu.SemaphoreType.DMA((nt,)),
            pltpu.SemaphoreType.DMA((2, 2, nc)),
            pltpu.SemaphoreType.DMA((1,)),
        ],
        compiler_params=pltpu.CompilerParams(
            collective_id=0, has_side_effects=True, vmem_limit_bytes=VMEM_LIMIT
        ),
        name="gather_project",
    )(wab, x)


def attention_kernel(nh, head_ref, slot_ref, base_ref, lr_ref, bt_ref, q_ref, v_ref, g_ref, lg_ref, gb_ref, qt, dpt):
    pair = pl.program_id(0)
    half = HEAD
    tokens = q_ref.shape[0]
    lo, hi = slice(0, half), slice(half, tokens)

    @pl.when(pair == 0)
    def _():
        for h in range(nh):
            cols = slice(h * HEAD, (h + 1) * HEAD)
            qt[h] = q_ref[:, cols].astype(F32).T.astype(BF16)
            dpt[h] = dot(v_ref[...], g_ref[:, cols], ((1,), (1,)))

    keep = lax.broadcasted_iota(jnp.int32, (half, half), 0) <= lax.broadcasted_iota(
        jnp.int32, (half, half), 1
    )
    lane = lax.broadcasted_iota(jnp.int32, (HEAD, HEAD), 1)
    lr = lr_ref[0]
    bt = bt_ref[0]
    bt32 = bt.astype(F32)
    b_rows = bt32.T.astype(BF16)
    base = base_ref[...].astype(F32)
    zero = jnp.zeros_like(bt32)
    for j in range(2):
        mine = jnp.where((lane >= RANK) == (j == 1), bt32, zero).astype(BF16)
        keys = (base + ADAPTER_SCALE * dot(lr, mine, ((1,), (1,)))).astype(BF16)
        total_lo = jnp.zeros((half, HEAD), F32)
        total_hi = jnp.zeros((half, HEAD), F32)
        for h in range(nh):
            cols = slice(h * HEAD, (h + 1) * HEAD)
            s_top = dot(keys[lo], qt[h])
            s_low = dot(keys[hi], qt[h, :, hi])
            a = jnp.where(keep, s_top[:, lo], -1e30)
            m = jnp.max(a, axis=0, keepdims=True)
            e = jnp.exp2((a - m) * EXP2_SCALE)
            inv = 1.0 / jnp.sum(e, axis=0, keepdims=True)
            dp = dpt[h, lo, lo]
            center = jnp.sum(e * dp, axis=0, keepdims=True) * inv
            d00 = (e * inv * (dp - center)).astype(BF16)
            a0 = s_top[:, hi]
            a1 = jnp.where(keep, s_low, -1e30)
            m = jnp.maximum(
                jnp.max(a0, axis=0, keepdims=True), jnp.max(a1, axis=0, keepdims=True)
            )
            e0 = jnp.exp2((a0 - m) * EXP2_SCALE)
            e1 = jnp.exp2((a1 - m) * EXP2_SCALE)
            inv = 1.0 / (jnp.sum(e0, axis=0, keepdims=True) + jnp.sum(e1, axis=0, keepdims=True))
            dp0 = dpt[h, lo, hi]
            dp1 = dpt[h, hi, hi]
            center = (
                jnp.sum(e0 * dp0, axis=0, keepdims=True) + jnp.sum(e1 * dp1, axis=0, keepdims=True)
            ) * inv
            d01 = (e0 * inv * (dp0 - center)).astype(BF16)
            d11 = (e1 * inv * (dp1 - center)).astype(BF16)
            total_lo += dot(jnp.concatenate([d00, d01], axis=1), q_ref[:, cols])
            total_hi += dot(d11, q_ref[hi, cols])
        kg = (jnp.concatenate([total_lo, total_hi], axis=0) * SCORE_SCALE).astype(BF16)
        rows = slice(j * RANK, (j + 1) * RANK)
        out = pl.ds(pl.multiple_of(slot_ref[2 * pair + j] * RANK, RANK), RANK)
        lg_ref[out, :] = (ADAPTER_SCALE * dot(b_rows[rows], kg, ((1,), (1,)))).astype(BF16)
        gb_ref[out, :] = (ADAPTER_SCALE * dot(lr, kg, ((0,), (0,)))[rows]).astype(BF16)


def attention(nc, head, slot_of, base, lr, bt, q, v, g):
    tokens = q.shape[0]
    nh = q.shape[1] // (nc * HEAD)
    rows = 2 * nc * RANK
    return pl.pallas_call(
        functools.partial(attention_kernel, nh),
        out_shape=(
            jax.ShapeDtypeStruct((rows, tokens), BF16),
            jax.ShapeDtypeStruct((rows, HEAD), BF16),
        ),
        grid_spec=pltpu.PrefetchScalarGridSpec(
            num_scalar_prefetch=2,
            grid=(nc,),
            in_specs=[
                pl.BlockSpec((tokens, HEAD), lambda i, hd, sl: (0, 0)),
                pl.BlockSpec((1, tokens, HEAD), lambda i, hd, sl: (i, 0, 0)),
                pl.BlockSpec((1, HEAD, HEAD), lambda i, hd, sl: (i, 0, 0)),
                pl.BlockSpec((tokens, nh * HEAD), lambda i, hd, sl: (0, hd[0])),
                pl.BlockSpec((tokens, HEAD), lambda i, hd, sl: (0, hd[0])),
                pl.BlockSpec((tokens, nh * HEAD), lambda i, hd, sl: (0, hd[0])),
            ],
            out_specs=(
                pl.BlockSpec((rows, tokens), lambda i, hd, sl: (0, 0)),
                pl.BlockSpec((rows, HEAD), lambda i, hd, sl: (0, 0)),
            ),
            scratch_shapes=[
                pltpu.VMEM((nh, HEAD, tokens), BF16),
                pltpu.VMEM((nh, tokens, tokens), F32),
            ],
        ),
        compiler_params=pltpu.CompilerParams(
            dimension_semantics=("arbitrary",), vmem_limit_bytes=VMEM_LIMIT
        ),
        name="attention",
    )(head, slot_of, base, lr, bt, q, v, g)


def scatter_kernel(
    nc, nt, donor_ref, lgp_ref, gb_ref, x_ref, kept_ref,
    a_ref, gbs_ref, b_ref,
    rc, part, sib, ring, ybuf, kept, piece, lg, csem, ksem, sibsem, ringsem, ysem, gsem,
):
    at = Place(nc, nt)
    nz, half = at.nz, at.nz // 2
    rb = x_ref.shape[1] // nt
    gr = gb_ref.shape[1]
    hg = gr // 2
    npb = nt // nc
    two = 2 * RANK
    left, right = (at.c, at.tok(0, -1)), (at.c, at.tok(0, 1))
    across, sibling = (at.c, at.tok(1, 0)), (at.c, at.tok(0, 0, True))
    peers = [(at.chain(i), at.t) for i in range(1, nc)]
    group = at.t // npb
    turned = [(group, at.c * npb + q) for q in range(npb)]
    is_me = [(group == at.c) & (at.c * npb + q == at.t) for q in range(npb)]
    entry_barrier(
        [left, right, across, sibling] + peers,
        [(dev, jnp.logical_not(me)) for dev, me in zip(turned, is_me)],
    )
    waits = []

    def remote(src, dst, ssem, rsem, dev):
        return pltpu.make_async_remote_copy(
            src_ref=src, dst_ref=dst, send_sem=ssem, recv_sem=rsem, device_id=dev, device_id_type=MESH
        )

    heads = []
    for i in range(1, nc):
        cp = remote(lgp_ref.at[at.chain(i)], rc.at[i], csem.at[0, i], csem.at[1, i], (at.chain(i), at.t))
        cp.start()
        heads.append(cp)
    total = lgp_ref[at.c].astype(F32)
    for i, cp in enumerate(heads):
        cp.wait_recv()
        total += rc[i + 1].astype(F32)
    lg[...] = total.astype(BF16)
    waits += heads

    def block(b):
        cols = pl.ds(pl.multiple_of(b * rb, rb), rb)
        part[b, pl.ds(0, two), :] = dot(lg[...], x_ref[:, cols]).astype(BF16)
        part[b, pl.ds(two, hg), pl.ds(0, HEAD)] = gb_ref[b, pl.ds(0, hg), :]
        part[b, pl.ds(two, hg), pl.ds(HEAD, HEAD)] = gb_ref[b, pl.ds(hg, hg), :]

    def place(i, core):
        z = lax.rem(at.z + lax.rem(i, nz) + half, nz)
        yh = lax.rem(1 - at.yh + i // nz, 2)
        return (yh * nz + z) * 2 + core

    def to_sibling(i, b):
        return remote(part.at[b], sib.at[i], sibsem.at[0, i], sibsem.at[1, i], sibling)

    def first(i, carry):
        b = place(i, 1 - at.k)
        block(b)
        to_sibling(i, b).start()
        return carry

    def second(i, carry):
        block(place(i, at.k))
        return carry

    lax.fori_loop(0, 2 * nz, first, 0)
    lax.fori_loop(0, 2 * nz, second, 0)

    for i in range(1, nc):
        cp = remote(kept_ref, kept.at[at.c], ksem.at[0, i], ksem.at[1, i], (at.chain(i), at.t))
        cp.start()
        waits.append(cp)
    kept[at.c] = kept_ref[...]

    def join(i, carry):
        b = place(i, at.k)
        to_sibling(i, b).wait()
        part[b] = (part[b].astype(F32) + sib[i].astype(F32)).astype(BF16)
        return carry

    lax.fori_loop(0, 2 * nz, join, 0)

    def hop(stream, way, s):
        reach = half if (stream + way) % 2 == 0 else half - 1
        if s > reach:
            return
        sign = 1 if way == 0 else -1
        b = at.tok(1 - stream, sign * (reach + 1 - s))
        if s > 1:
            link(stream, way, s - 1).wait_recv()
            part[b] = (part[b].astype(F32) + ring[stream, way, s - 2].astype(F32)).astype(BF16)
        cp = link(stream, way, s, b)
        cp.start()
        waits_send.append(cp)

    waits_send = []

    def link(stream, way, s, b=0):
        return remote(
            part.at[b],
            ring.at[stream, way, s - 1],
            ringsem.at[0, stream, way, s - 1],
            ringsem.at[1, stream, way, s - 1],
            right if way == 0 else left,
        )

    def finish(stream):
        b = at.tok(1 - stream, 0)
        value = part[b].astype(F32)
        for way in range(2):
            reach = half if (stream + way) % 2 == 0 else half - 1
            link(stream, way, reach).wait_recv()
            value += ring[stream, way, reach - 1].astype(F32)
        return b, value

    for s in range(1, half + 1):
        for stream in range(2):
            for way in range(2):
                hop(stream, way, s)
    b, value = finish(0)
    part[b] = value.astype(BF16)
    cross = remote(part.at[b], ybuf, ysem.at[0], ysem.at[1], across)
    cross.start()
    b, value = finish(1)
    cross.wait()
    value += ybuf[...].astype(F32)

    piece[pl.ds(0, hg), :] = value[two:, :HEAD]
    piece[pl.ds(hg, hg), :] = value[two:, HEAD:]
    slot = lax.rem(at.t, npb)
    for q in range(npb):
        cp = remote(piece, gbs_ref.at[slot], gsem.at[0, q], gsem.at[1, slot], turned[q])
        local = pltpu.make_async_copy(piece, gbs_ref.at[slot], gsem.at[1, slot])

        @pl.when(jnp.logical_not(is_me[q]))
        def _():
            cp.start()

        @pl.when(is_me[q])
        def _():
            local.start()

    for cp in waits:
        cp.wait_send()
    for i in range(1, nc):
        remote(kept_ref, kept.at[0], ksem.at[0, i], ksem.at[1, i], sibling).wait_recv()
    for j in range(2):
        whole = kept[donor_ref[j]]
        odd = donor_ref[2 + j] == 1
        rows = slice(j * RANK, (j + 1) * RANK)
        mine = jnp.where(odd, whole[RANK:two], whole[:RANK])
        a_ref[rows, :] = mine - STRIDE_LENGTH * value[rows]
        b_ref[j] = whole[two:]
    for cp in waits_send:
        cp.wait_send()
    for q in range(npb):
        pltpu.make_async_copy(piece, gbs_ref.at[q], gsem.at[1, q]).wait()
        cp = remote(piece, gbs_ref.at[slot], gsem.at[0, q], gsem.at[1, slot], turned[q])

        @pl.when(jnp.logical_not(is_me[q]))
        def _():
            cp.wait_send()


def scatter(nc, nt, donor, lgp, gb, x, kept):
    tokens = x.shape[0]
    rb = x.shape[1] // nt
    nz = nt // 4
    gr = gb.shape[1]
    rows = 2 * RANK + gr // 2
    krows = kept.shape[0]
    vmem = pl.BlockSpec(memory_space=pltpu.VMEM)
    sem = pltpu.SemaphoreType.DMA
    return pl.pallas_call(
        functools.partial(scatter_kernel, nc, nt),
        out_shape=(
            jax.ShapeDtypeStruct((2 * RANK, rb), F32),
            jax.ShapeDtypeStruct((nt // nc, gr, HEAD), F32),
            jax.ShapeDtypeStruct((2, krows - 2 * RANK, 2 * HEAD), F32),
        ),
        in_specs=[pl.BlockSpec(memory_space=pltpu.SMEM)] + [vmem] * 4,
        out_specs=(vmem,) * 3,
        scratch_shapes=[
            pltpu.VMEM((nc, 2 * RANK, tokens), BF16),
            pltpu.VMEM((nt, rows, rb), BF16),
            pltpu.VMEM((nt // 2, rows, rb), BF16),
            pltpu.VMEM((2, 2, nz // 2, rows, rb), BF16),
            pltpu.VMEM((rows, rb), BF16),
            pltpu.VMEM((nc, krows, rb), F32),
            pltpu.VMEM((gr, HEAD), F32),
            pltpu.VMEM((2 * RANK, tokens), BF16),
            sem((2, nc)),
            sem((2, nc)),
            sem((2, nt // 2)),
            sem((2, 2, 2, nz // 2)),
            sem((2,)),
            sem((2, nt // nc)),
        ],
        compiler_params=pltpu.CompilerParams(
            collective_id=1, has_side_effects=True, vmem_limit_bytes=VMEM_LIMIT
        ),
        name="scatter_sum",
    )(donor, lgp, gb, x, kept)


def per_device(nc, nt, x, q, v, g, w, first, second, first_noise, second_noise, heats, donor):
    c = lax.axis_index("chain").astype(jnp.int32)
    t = lax.axis_index("tok").astype(jnp.int32)
    rb = first.shape[1]
    cb = second.shape[2]
    bt = second.astype(BF16).reshape(2 * RANK, cb).T
    wab = jnp.concatenate(
        [
            jnp.concatenate([w, first[0].astype(BF16), first[1].astype(BF16)], axis=1),
            jnp.concatenate([bt[: cb // 2], bt[cb // 2 :]], axis=1),
        ],
        axis=0,
    )
    base, lr, btall = gather_and_project(nc, nt, wab, x)

    chains = jnp.arange(2 * nc, dtype=jnp.int32)
    slot_of = jnp.sum(jnp.where(donor[:, None] == chains[None, :], chains[:, None], 0), axis=0)
    lg, gb = attention(nc, c[None], slot_of, base, lr, btall, q, v, g)

    heat = jnp.sqrt(2.0 * STRIDE_LENGTH * heats)[:, None, None]
    kept_a = (1.0 - STRIDE_LENGTH) * first + heat * first_noise
    kept_b = (1.0 - STRIDE_LENGTH) * second + heat * second_noise
    kept = jnp.concatenate(
        [
            kept_a.transpose(0, 2, 1).reshape(2 * RANK, rb),
            kept_b.reshape(2 * RANK * cb // rb, rb),
        ],
        axis=0,
    )
    mine = lax.dynamic_slice(donor, (2 * c,), (2,))
    source = jnp.concatenate([mine // 2, mine % 2])
    new_at, gbs, kept_pair = scatter(
        nc,
        nt,
        source,
        lg.reshape(nc, 2 * RANK, x.shape[0]),
        gb.reshape(nt, 2 * nc * RANK // nt, HEAD),
        x,
        kept,
    )
    new_a = new_at.reshape(2, RANK, rb).transpose(0, 2, 1)
    kept_pair = kept_pair.reshape(2, 2, RANK, cb)
    odd = (mine % 2 == 1)[:, None, None]
    kept_mine = jnp.where(odd, kept_pair[:, 1], kept_pair[:, 0])
    column = lax.rem(t, nt // nc) * cb
    sums = lax.dynamic_slice(gbs.reshape(2, RANK, HEAD), (0, 0, column), (2, RANK, cb))
    return new_a, kept_mine - STRIDE_LENGTH * sums


def solution(mesh):
    return jax.shard_map(
        functools.partial(per_device, mesh.shape["chain"], mesh.shape["tok"]),
        mesh=mesh,
        in_specs=(
            P("tok", None),
            P("tok", None),
            P("tok", None),
            P("tok", None),
            P("tok", "chain"),
            P("chain", "tok", None),
            P("chain", None, "tok"),
            P("chain", "tok", None),
            P("chain", None, "tok"),
            P("chain"),
            P(),
        ),
        out_specs=(P("chain", "tok", None), P("chain", None, "tok")),
        check_vma=False,
    )
```

```python
import functools
import math

import jax
import jax.numpy as jnp
from jax import lax
from jax.experimental import pallas as pl
from jax.experimental.pallas import tpu as pltpu
from jax.sharding import PartitionSpec as P

MESH = pl.DeviceIdType.MESH
HEAD = 128
RANK = 64
MODEL_WIDTH = 8192
STRIDE_LENGTH = 0.2
ADAPTER_SCALE = 1.0 / math.sqrt(MODEL_WIDTH * RANK)
SCORE_SCALE = 1.0 / math.sqrt(HEAD)
EXP2_SCALE = SCORE_SCALE * math.log2(math.e)
VMEM_LIMIT = 56 * 1024 * 1024

F32 = jnp.float32
BF16 = jnp.bfloat16


def dot(a, b, dims=((1,), (0,))):
    return lax.dot_general(a, b, (dims, ((), ())), preferred_element_type=F32)


class Place:
    def __init__(self, nc, nt):
        self.nc, self.nt, self.nz = nc, nt, nt // 4
        self.c = lax.axis_index("chain")
        self.t = lax.axis_index("tok")
        self.k = lax.rem(self.t, 2)
        self.z = lax.rem(self.t // 2, self.nz)
        self.yh = self.t // (2 * self.nz)

    def tok(self, other_yh, dz, other_k=False):
        yh = 1 - self.yh if other_yh else self.yh
        k = 1 - self.k if other_k else self.k
        z = lax.rem(self.z + (dz + self.nz), self.nz)
        return (yh * self.nz + z) * 2 + k

    def chain(self, i):
        return lax.rem(self.c + i, self.nc)


def entry_barrier(devices, extra=()):
    barrier = pltpu.get_barrier_semaphore()
    for dev in devices:
        pl.semaphore_signal(barrier, inc=1, device_id=dev, device_id_type=MESH)
    count = len(devices)
    for dev, present in extra:

        @pl.when(present)
        def _():
            pl.semaphore_signal(barrier, inc=1, device_id=dev, device_id_type=MESH)

        count = count + present.astype(jnp.int32)
    pl.semaphore_wait(barrier, count)


def routes(nz):
    half, near = nz // 2, nz // 4
    far = [d for d in range(-(half - 1), half + 1) if abs(d) > near]
    return half, near, far


def remote(src, dst, ssem, rsem, dev):
    return pltpu.make_async_remote_copy(
        src_ref=src, dst_ref=dst, send_sem=ssem, recv_sem=rsem, device_id=dev, device_id_type=MESH
    )


def gather_kernel(
    nc, nt, w_ref, first_ref, second_ref, x_hbm,
    base_ref, lr_ref, bt_ref,
    fa, fw, x_ref, acc, ssem, rsem, csem, xsem,
):
    at = Place(nc, nt)
    half, near, far = routes(at.nz)
    rb = w_ref.shape[0]
    cb = second_ref.shape[2]
    npb = nt // nc
    me = at.t
    left, right = (at.c, at.tok(0, -1)), (at.c, at.tok(0, 1))
    across, sibling = (at.c, at.tok(1, 0)), (at.c, at.tok(0, 0, True))
    load = pltpu.make_async_copy(x_hbm, x_ref, xsem.at[0])
    load.start()
    fa[me, pl.ds(0, rb), :] = jnp.concatenate([first_ref[0], first_ref[1]], axis=1).astype(BF16)
    fa[me, pl.ds(rb, cb), :] = jnp.concatenate([second_ref[0], second_ref[1]], axis=0).T.astype(BF16)
    fw[me] = w_ref[...]
    entry_barrier([left, right, across, sibling] + [(at.chain(i), at.t) for i in range(1, nc)])
    full = (fa, fw)
    sends = []

    def send(kind, b, dev):
        cp = remote(full[kind].at[b], full[kind].at[b], ssem.at[len(sends)], rsem.at[kind, b], dev)
        cp.start()
        sends.append(cp)

    def wait(kind, b):
        remote(full[kind].at[b], full[kind].at[b], ssem.at[0], rsem.at[kind, b], sibling).wait_recv()

    def product(kind, b):
        cols = pl.ds(pl.multiple_of(b * rb, rb), rb)
        acc[kind] += dot(x_ref[:, cols], full[kind][b, pl.ds(0, rb), :])

    groups = []
    for s in range(1, half + 1):
        group = []
        for way, onward, reach in ((-1, right, half), (1, left, half - 1)):
            if s <= reach:
                nxt = [onward] if s < reach else []
                if way * s in far or -way * s in far and s == half:
                    nxt = nxt + [across]
                group.append((0, way * s, nxt))
        if s == 1:
            group.append((1, 0, [right, left]))
        elif s - 1 <= near:
            for way, onward in ((-1, right), (1, left)):
                group.append((1, way * (s - 1), [onward] if s - 1 < near else []))
        groups.append(group)
    groups[-1] += [(1, d, []) for d in far if abs(d) < half]
    groups.append([(1, half, [])])

    def arrive(kind, group):
        blocks = []
        for other_yh, dz, nxt in group:
            b = at.tok(other_yh, dz)
            wait(kind, b)
            for dev in nxt:
                send(kind, b, dev)
            send(kind, b, sibling)
            blocks.append(b)
        for b in blocks:
            product(kind, b)

    def twins(kind, group):
        for other_yh, dz, _ in group:
            b = at.tok(other_yh, dz, True)
            wait(kind, b)
            product(kind, b)

    own = [(0, 0, [])]
    for kind in range(2):
        for dev in (right, left, across, sibling):
            send(kind, me, dev)
    acc[...] = jnp.zeros_like(acc)
    load.wait()
    product(0, me)
    product(1, me)
    last = len(groups)
    arrive(0, groups[0])
    twins(0, own)
    for g in range(1, last):
        arrive(0, groups[g])
        twins(0, groups[g - 1])
        if g < last - 1:
            arrive(1, groups[g - 1])
    twins(0, groups[last - 1])

    exchanges = []

    def exchange(src, dst, i, kind):
        cp = remote(src, dst, csem.at[kind, 0, i], csem.at[kind, 1, i], (at.chain(i), at.t))
        cp.start()
        exchanges.append(cp)

    lr_ref[at.c] = acc[0].astype(BF16)
    for i in range(1, nc):
        exchange(lr_ref.at[at.c], lr_ref.at[at.c], i, 1)
    for i in range(1, nc):
        exchange(fa.at[pl.ds(at.chain(i) * npb, npb), pl.ds(rb, cb), :], bt_ref.at[at.c], i, 0)
    for u in range(npb):
        bt_ref[at.c, u] = fa[at.c * npb + u, pl.ds(rb, cb), :]

    twins(1, own)
    for g in range(last - 2):
        twins(1, groups[g])
    for g in range(last - 2, last):
        arrive(1, groups[g])
        twins(1, groups[g])
    base_ref[...] = acc[1].astype(BF16)
    for cp in exchanges:
        cp.wait()
    for cp in sends:
        cp.wait_send()


def gather_and_project(nc, nt, w, first, second, x):
    tokens = x.shape[0]
    rb, cb = w.shape[0], second.shape[2]
    npb = nt // nc
    vmem = pl.BlockSpec(memory_space=pltpu.VMEM)
    return pl.pallas_call(
        functools.partial(gather_kernel, nc, nt),
        out_shape=(
            jax.ShapeDtypeStruct((tokens, HEAD), BF16),
            jax.ShapeDtypeStruct((nc, tokens, HEAD), BF16),
            jax.ShapeDtypeStruct((nc, npb, cb, HEAD), BF16),
        ),
        in_specs=[vmem] * 3 + [pl.BlockSpec(memory_space=pl.ANY)],
        out_specs=(vmem,) * 3,
        scratch_shapes=[
            pltpu.VMEM((nt, rb + cb, HEAD), BF16),
            pltpu.VMEM((nt, rb, HEAD), BF16),
            pltpu.VMEM(x.shape, BF16),
            pltpu.VMEM((2, tokens, HEAD), F32),
            pltpu.SemaphoreType.DMA((4 * nt,)),
            pltpu.SemaphoreType.DMA((2, nt)),
            pltpu.SemaphoreType.DMA((2, 2, nc)),
            pltpu.SemaphoreType.DMA((1,)),
        ],
        compiler_params=pltpu.CompilerParams(
            collective_id=0, has_side_effects=True, vmem_limit_bytes=VMEM_LIMIT
        ),
        name="gather_project",
    )(w, first, second, x)


def softmax_part(nh, s_top, s_low, dp_top, dp_low, d_top, d_low):
    half, early = HEAD, nh * HEAD
    keep = lax.broadcasted_iota(jnp.int32, (half, half), 0) <= lax.broadcasted_iota(
        jnp.int32, (half, half), 1
    )
    for j in range(2):
        rows = slice(j * half, (j + 1) * half)
        for h in range(nh):
            cols = slice(h * HEAD, (h + 1) * HEAD)
            back = slice(early + h * HEAD, early + (h + 1) * HEAD)
            a = jnp.where(keep, s_top[rows, cols], -1e30)
            m = jnp.max(a, axis=0, keepdims=True)
            e = jnp.exp2((a - m) * EXP2_SCALE)
            inv = 1.0 / jnp.sum(e, axis=0, keepdims=True)
            dp = dp_top[:, cols]
            center = jnp.sum(e * dp, axis=0, keepdims=True) * inv
            d_top[rows, cols] = (e * inv * (dp - center)).astype(BF16)
            a0 = s_top[rows, back]
            a1 = jnp.where(keep, s_low[rows, cols], -1e30)
            m = jnp.maximum(
                jnp.max(a0, axis=0, keepdims=True), jnp.max(a1, axis=0, keepdims=True)
            )
            e0 = jnp.exp2((a0 - m) * EXP2_SCALE)
            e1 = jnp.exp2((a1 - m) * EXP2_SCALE)
            inv = 1.0 / (jnp.sum(e0, axis=0, keepdims=True) + jnp.sum(e1, axis=0, keepdims=True))
            dp0 = dp_top[:, back]
            dp1 = dp_low[:, cols]
            center = (
                jnp.sum(e0 * dp0, axis=0, keepdims=True) + jnp.sum(e1 * dp1, axis=0, keepdims=True)
            ) * inv
            d_top[rows, back] = (e0 * inv * (dp0 - center)).astype(BF16)
            d_low[rows, cols] = (e1 * inv * (dp1 - center)).astype(BF16)


def back_kernel(
    nc, nt, donor_ref, heat_ref, base_ref, lr_ref, bt_ref, first_ref, second_ref, noise_ref, noise_b_ref,
    q_hbm, v_hbm, g_hbm, x_hbm,
    a_ref, b_ref,
    q_ref, v_ref, g_ref, x_ref, qt, qr, dp_top, dp_low, s_top, s_low, d_top, d_low,
    lgp, gb, rc, part, sib, ring, far_in, ybuf, kept_a, kept_b, piece, gbs, turn, lg,
    loadsem, csem, ksem, sibsem, ringsem, ysem, gsem,
):
    at = Place(nc, nt)
    half, near, far = routes(at.nz)
    tokens = base_ref.shape[0]
    rb = first_ref.shape[1]
    cb = second_ref.shape[2]
    gr = gb.shape[1]
    hg = gr // 2
    npb = nt // nc
    nh = q_ref.shape[1] // HEAD
    early = nh * HEAD
    two = 2 * RANK
    lo, hi = slice(0, HEAD), slice(HEAD, tokens)
    left, right = (at.c, at.tok(0, -1)), (at.c, at.tok(0, 1))
    across, sibling = (at.c, at.tok(1, 0)), (at.c, at.tok(0, 0, True))
    group = at.t // npb
    turned = [(group, at.c * npb + q) for q in range(npb)]
    is_me = [(group == at.c) & (at.c * npb + q == at.t) for q in range(npb)]

    wide = pl.ds(pl.multiple_of(at.c * early, HEAD), early)
    narrow = pl.ds(pl.multiple_of(at.c * HEAD, HEAD), HEAD)
    loads = [
        pltpu.make_async_copy(q_hbm.at[:, wide], q_ref, loadsem.at[0]),
        pltpu.make_async_copy(v_hbm.at[:, narrow], v_ref, loadsem.at[1]),
        pltpu.make_async_copy(g_hbm.at[:, wide], g_ref, loadsem.at[2]),
        pltpu.make_async_copy(x_hbm, x_ref, loadsem.at[3]),
    ]
    for cp in loads:
        cp.start()

    me_c = at.c
    for j in range(2):
        heat = jnp.sqrt(jnp.full((1, rb), 2.0 * STRIDE_LENGTH * heat_ref[j], F32))
        kept = (1.0 - STRIDE_LENGTH) * first_ref[j].T + heat * noise_ref[j].T
        kept_a[me_c, j * RANK : (j + 1) * RANK, :] = kept
    rows_b = jnp.concatenate(
        [
            (1.0 - STRIDE_LENGTH) * second_ref[j]
            + jnp.sqrt(jnp.full((1, cb), 2.0 * STRIDE_LENGTH * heat_ref[j], F32)) * noise_b_ref[j]
            for j in range(2)
        ],
        axis=0,
    )
    kept_b[me_c] = rows_b.T
    entry_barrier(
        [left, right, across, sibling] + [(at.chain(i), at.t) for i in range(1, nc)],
        [(dev, jnp.logical_not(me)) for dev, me in zip(turned, is_me)],
    )
    swaps = []
    for i in range(1, nc):
        dev = (at.chain(i), at.t)
        swaps.append(remote(kept_a.at[me_c], kept_a.at[me_c], ksem.at[0, 0, i], ksem.at[0, 1, i], dev))
        swaps.append(remote(kept_b.at[me_c], kept_b.at[me_c], ksem.at[1, 0, i], ksem.at[1, 1, i], dev))
    for cp in swaps:
        cp.start()

    for cp in loads[:3]:
        cp.wait()
    for h in range(nh):
        cols = slice(h * HEAD, (h + 1) * HEAD)
        later = slice(early + h * HEAD, early + (h + 1) * HEAD)
        q_t = q_ref[:, cols].astype(F32).T.astype(BF16)
        qt[:, cols] = q_t[:, lo]
        qt[:, later] = q_t[:, hi]
        qr[cols] = q_ref[lo, cols]
        qr[later] = q_ref[hi, cols]
        top = dot(v_ref[lo], g_ref[:, cols], ((1,), (1,)))
        dp_top[:, cols] = top[:, lo]
        dp_top[:, later] = top[:, hi]
        dp_low[:, cols] = dot(v_ref[hi], g_ref[hi, cols], ((1,), (1,)))

    lane = lax.broadcasted_iota(jnp.int32, (HEAD, HEAD), 1)

    def heads_of(i):
        return remote(
            lgp.at[at.chain(i)], rc.at[i], csem.at[0, i], csem.at[1, i], (at.chain(i), at.t)
        )

    def pair(p):
        keys, factors = [], []
        base = base_ref[...].astype(F32)
        for j in range(2):
            chain = donor_ref[2 * p + j]
            source = lax.shift_right_logical(chain, 1)
            odd = lax.bitwise_and(chain, 1)
            lr = lr_ref[source]
            bt = bt_ref[source].reshape(HEAD, HEAD).astype(F32)
            upper = (lane >= RANK).astype(jnp.int32)
            mine = jnp.where(upper == odd, bt, jnp.zeros_like(bt))
            keys.append((base + ADAPTER_SCALE * dot(lr, mine.astype(BF16), ((1,), (1,)))).astype(BF16))
            factors.append((odd == 1, lr, bt.T))
        s_top[...] = dot(jnp.concatenate([keys[0][lo], keys[1][lo]], axis=0), qt[...])
        s_low[...] = dot(jnp.concatenate([keys[0][hi], keys[1][hi]], axis=0), qt[:, early:])
        softmax_part(nh, s_top, s_low, dp_top, dp_low, d_top, d_low)
        kg_lo = (dot(d_top[...], qr[...]) * SCORE_SCALE).astype(BF16)
        kg_hi = (dot(d_low[...], qr[early:]) * SCORE_SCALE).astype(BF16)
        for j in range(2):
            odd, lr, b_rows = factors[j]
            here = slice(j * HEAD, (j + 1) * HEAD)
            kg = jnp.concatenate([kg_lo[here], kg_hi[here]], axis=0)
            b_mine = jnp.where(odd, b_rows[RANK:], b_rows[:RANK]).astype(BF16)
            lgp[p, j * RANK : (j + 1) * RANK, :] = (
                ADAPTER_SCALE * dot(b_mine, kg, ((1,), (1,)))
            ).astype(BF16)
            both = dot(lr, kg, ((0,), (0,)))
            grad_b = (ADAPTER_SCALE * jnp.where(odd, both[RANK:], both[:RANK])).astype(BF16)
            per = RANK // gr
            for u in range(per):
                gb[(2 * p + j) * per + u] = grad_b[u * gr : (u + 1) * gr]

    def peer_pair(i, carry):
        pair(at.chain(i))

        @pl.when(i < nc)
        def _():
            heads_of(i).start()

        return carry

    lax.fori_loop(1, nc + 1, peer_pair, 0)

    total = lgp[at.c].astype(F32)
    for i in range(1, nc):
        heads_of(i).wait_recv()
        total += rc[i].astype(F32)
    lg[...] = total.astype(BF16)
    loads[3].wait()

    order = [(1, d) for d in sorted(far, key=lambda d: -abs(d))]
    order += [(0, d) for d in sorted(far, key=lambda d: -abs(d))]
    for m in range(near, 0, -1):
        order += [(1, -m), (1, m), (0, -m), (0, m)]
    order += [(1, 0), (0, 0)]
    rank_of = {dest: i for i, dest in enumerate(order)}

    def block(b):
        cols = pl.ds(pl.multiple_of(b * rb, rb), rb)
        second = jnp.concatenate([gb[b, pl.ds(0, hg), :], gb[b, pl.ds(hg, hg), :]], axis=1)
        return dot(lg[...], x_ref[:, cols]), second

    def to_sibling(i, b):
        return remote(part.at[b], sib.at[i], sibsem.at[0, i], sibsem.at[1, i], sibling)

    sent = []
    for i, (other_yh, dz) in enumerate(order):
        b = at.tok(other_yh, dz, True)
        first, second = block(b)
        part[b, pl.ds(0, two), :] = first.astype(BF16)
        part[b, pl.ds(two, hg), :] = second
        cp = to_sibling(i, b)
        cp.start()
        sent.append(cp)

    def join(other_yh, dz):
        i = rank_of[other_yh, dz]
        b = at.tok(other_yh, dz)
        first, second = block(b)
        sent[i].wait_recv()
        part[b, pl.ds(0, two), :] = (first + sib[i, pl.ds(0, two), :].astype(F32)).astype(BF16)
        part[b, pl.ds(two, hg), :] = (
            second.astype(F32) + sib[i, pl.ds(two, hg), :].astype(F32)
        ).astype(BF16)
        return b

    def far_copy(dz):
        i = far.index(dz)
        return remote(
            part.at[at.tok(1, dz)], far_in.at[i], ysem.at[0, i], ysem.at[1, i], across
        )

    reach = {(0, 0): half, (0, 1): half - 1, (1, 0): near, (1, 1): near}

    def link(other_yh, way, s, b):
        return remote(
            part.at[b],
            ring.at[other_yh, way, s - 1],
            ringsem.at[0, other_yh, way, s - 1],
            ringsem.at[1, other_yh, way, s - 1],
            right if way == 0 else left,
        )

    def hop(other_yh, way, s):
        far_reach = reach[other_yh, way]
        dz = (far_reach + 1 - s) * (1 if way == 0 else -1)
        b = at.tok(other_yh, dz)
        adds = []
        if other_yh == 0 and dz in far:
            far_copy(dz).wait_recv()
            adds.append(far_in[far.index(dz)].astype(F32))
        if s > 1:
            link(other_yh, way, s - 1, b).wait_recv()
            adds.append(ring[other_yh, way, s - 2].astype(F32))
        if adds:
            value = part[b].astype(F32)
            for term in adds:
                value += term
            part[b] = value.astype(BF16)
        cp = link(other_yh, way, s, b)
        cp.start()
        sent.append(cp)

    def arrived(other_yh, b):
        value = part[b].astype(F32)
        for way in range(2):
            last = reach[other_yh, way]
            if last:
                link(other_yh, way, last, b).wait_recv()
                value += ring[other_yh, way, last - 1].astype(F32)
        return value

    for other_yh, dz in order:
        if other_yh == 1 and dz in far:
            join(1, dz)
            cp = far_copy(dz)
            cp.start()
            sent.append(cp)
    for other_yh, dz in order:
        if other_yh == 0 and dz in far:
            join(0, dz)
    for s in range(1, half + 1):
        m = near + 1 - s
        if m >= 1:
            join(1, m)
            hop(1, 0, s)
            join(1, -m)
            hop(1, 1, s)
        for way in range(2):
            if s <= reach[0, way]:
                dz = (reach[0, way] + 1 - s) * (1 if way == 0 else -1)
                if dz not in far:
                    join(0, dz)
                hop(0, way, s)
        if m == 0:
            b = join(1, 0)
            part[b] = arrived(1, b).astype(BF16)
            cross = remote(part.at[b], ybuf, ysem.at[0, len(far)], ysem.at[1, len(far)], across)
            cross.start()
    b = join(0, 0)
    value = arrived(0, b)
    cross.wait()
    value += ybuf[...].astype(F32)

    piece[pl.ds(0, hg), :] = value[two:, :HEAD]
    piece[pl.ds(hg, hg), :] = value[two:, HEAD:]
    slot = lax.rem(at.t, npb)
    for q in range(npb):
        cp = remote(piece, gbs.at[slot], gsem.at[0, q], gsem.at[1, slot], turned[q])
        local = pltpu.make_async_copy(piece, gbs.at[slot], gsem.at[1, slot])

        @pl.when(jnp.logical_not(is_me[q]))
        def _():
            cp.start()

        @pl.when(is_me[q])
        def _():
            local.start()

    for cp in swaps:
        cp.wait()
    kept_t = []
    for j in range(2):
        chain = donor_ref[2 * at.c + j]
        source = lax.shift_right_logical(chain, 1)
        odd = lax.bitwise_and(chain, 1) == 1
        whole = kept_a[source]
        rows = slice(j * RANK, (j + 1) * RANK)
        mine = jnp.where(odd, whole[RANK:], whole[:RANK]) - STRIDE_LENGTH * value[rows]
        a_ref[j] = mine.T
        columns = kept_b[source].T
        kept_t.append(jnp.where(odd, columns[RANK:], columns[:RANK]))
    for cp in sent:
        cp.wait_send()
    for i in range(1, nc):
        heads_of(i).wait_send()
    for q in range(npb):
        pltpu.make_async_copy(piece, gbs.at[q], gsem.at[1, q]).wait()
        cp = remote(piece, gbs.at[slot], gsem.at[0, q], gsem.at[1, slot], turned[q])

        @pl.when(jnp.logical_not(is_me[q]))
        def _():
            cp.wait_send()

    turn[...] = jnp.concatenate([gbs[q] for q in range(npb)], axis=0).T
    sums = turn[pl.ds(pl.multiple_of(slot * cb, cb), cb), :].T
    for j in range(2):
        b_ref[j] = kept_t[j] - STRIDE_LENGTH * sums[j * RANK : (j + 1) * RANK]


def back(nc, nt, donor, heats, base, lr, bt, first, second, noise, noise_b, q, v, g, x):
    tokens = x.shape[0]
    rb, cb = first.shape[1], second.shape[2]
    nz = nt // 4
    half, near, far = routes(nz)
    nh = q.shape[1] // (nc * HEAD)
    gr = 2 * nc * RANK // nt
    rows = 2 * RANK + gr // 2
    vmem = pl.BlockSpec(memory_space=pltpu.VMEM)
    smem = pl.BlockSpec(memory_space=pltpu.SMEM)
    hbm = pl.BlockSpec(memory_space=pl.ANY)
    sem = pltpu.SemaphoreType.DMA
    return pl.pallas_call(
        functools.partial(back_kernel, nc, nt),
        out_shape=(
            jax.ShapeDtypeStruct(first.shape, F32),
            jax.ShapeDtypeStruct(second.shape, F32),
        ),
        in_specs=[smem] * 2 + [vmem] * 7 + [hbm] * 4,
        out_specs=(vmem,) * 2,
        scratch_shapes=[
            pltpu.VMEM((tokens, nh * HEAD), BF16),
            pltpu.VMEM((tokens, HEAD), BF16),
            pltpu.VMEM((tokens, nh * HEAD), BF16),
            pltpu.VMEM(x.shape, BF16),
            pltpu.VMEM((HEAD, nh * tokens), BF16),
            pltpu.VMEM((nh * tokens, HEAD), BF16),
            pltpu.VMEM((HEAD, nh * tokens), F32),
            pltpu.VMEM((HEAD, nh * HEAD), F32),
            pltpu.VMEM((2 * HEAD, nh * tokens), F32),
            pltpu.VMEM((2 * HEAD, nh * HEAD), F32),
            pltpu.VMEM((2 * HEAD, nh * tokens), BF16),
            pltpu.VMEM((2 * HEAD, nh * HEAD), BF16),
            pltpu.VMEM((nc, 2 * RANK, tokens), BF16),
            pltpu.VMEM((nt, gr, HEAD), BF16),
            pltpu.VMEM((nc, 2 * RANK, tokens), BF16),
            pltpu.VMEM((nt, rows, rb), BF16),
            pltpu.VMEM((nt // 2, rows, rb), BF16),
            pltpu.VMEM((2, 2, half, rows, rb), BF16),
            pltpu.VMEM((len(far), rows, rb), BF16),
            pltpu.VMEM((rows, rb), BF16),
            pltpu.VMEM((nc, 2 * RANK, rb), F32),
            pltpu.VMEM((nc, cb, HEAD), F32),
            pltpu.VMEM((gr, HEAD), F32),
            pltpu.VMEM((nt // nc, gr, HEAD), F32),
            pltpu.VMEM((HEAD, HEAD), F32),
            pltpu.VMEM((2 * RANK, tokens), BF16),
            sem((4,)),
            sem((2, nc)),
            sem((2, 2, nc)),
            sem((2, nt // 2)),
            sem((2, 2, 2, half)),
            sem((2, len(far) + 1)),
            sem((2, nt // nc)),
        ],
        compiler_params=pltpu.CompilerParams(
            collective_id=1, has_side_effects=True, vmem_limit_bytes=VMEM_LIMIT
        ),
        name="attend_scatter",
    )(donor, heats, base, lr, bt, first, second, noise, noise_b, q, v, g, x)


def per_device(nc, nt, x, q, v, g, w, first, second, noise, noise_b, heats, donor):
    base, lr, bt = gather_and_project(nc, nt, w, first, second, x)
    return back(nc, nt, donor, heats, base, lr, bt, first, second, noise, noise_b, q, v, g, x)


def solution(mesh):
    return jax.shard_map(
        functools.partial(per_device, mesh.shape["chain"], mesh.shape["tok"]),
        mesh=mesh,
        in_specs=(
            P("tok", None),
            P("tok", None),
            P("tok", None),
            P("tok", None),
            P("tok", "chain"),
            P("chain", "tok", None),
            P("chain", None, "tok"),
            P("chain", "tok", None),
            P("chain", None, "tok"),
            P("chain"),
            P(),
        ),
        out_specs=(P("chain", "tok", None), P("chain", None, "tok")),
        check_vma=False,
    )
```

```python
import functools
import math

import jax
import jax.numpy as jnp
from jax import lax
from jax.experimental import pallas as pl
from jax.experimental.pallas import tpu as pltpu
from jax.sharding import PartitionSpec as P

MESH = pl.DeviceIdType.MESH
HEAD = 128
RANK = 64
MODEL_WIDTH = 8192
STRIDE_LENGTH = 0.2
ADAPTER_SCALE = 1.0 / math.sqrt(MODEL_WIDTH * RANK)
SCORE_SCALE = 1.0 / math.sqrt(HEAD)
EXP2_SCALE = SCORE_SCALE * math.log2(math.e)
VMEM_LIMIT = 56 * 1024 * 1024

F32 = jnp.float32
BF16 = jnp.bfloat16


def dot(a, b, dims=((1,), (0,))):
    return lax.dot_general(a, b, (dims, ((), ())), preferred_element_type=F32)


class Place:
    def __init__(self, nc, nt):
        self.nc, self.nt, self.nz = nc, nt, nt // 4
        self.c = lax.axis_index("chain")
        self.t = lax.axis_index("tok")
        self.k = lax.rem(self.t, 2)
        self.z = lax.rem(self.t // 2, self.nz)
        self.yh = self.t // (2 * self.nz)

    def tok(self, other_yh, dz, other_k=False):
        yh = 1 - self.yh if other_yh else self.yh
        k = 1 - self.k if other_k else self.k
        z = lax.rem(self.z + (dz + self.nz), self.nz)
        return (yh * self.nz + z) * 2 + k

    def chain(self, i):
        return lax.rem(self.c + i, self.nc)


def entry_barrier(devices, extra=()):
    barrier = pltpu.get_barrier_semaphore()
    for dev in devices:
        pl.semaphore_signal(barrier, inc=1, device_id=dev, device_id_type=MESH)
    count = len(devices)
    for dev, present in extra:

        @pl.when(present)
        def _():
            pl.semaphore_signal(barrier, inc=1, device_id=dev, device_id_type=MESH)

        count = count + present.astype(jnp.int32)
    pl.semaphore_wait(barrier, count)


def routes(nz):
    half, near = nz // 2, nz // 4
    far = [d for d in range(-(half - 1), half + 1) if abs(d) > near]
    return half, near, far


def remote(src, dst, ssem, rsem, dev):
    return pltpu.make_async_remote_copy(
        src_ref=src, dst_ref=dst, send_sem=ssem, recv_sem=rsem, device_id=dev, device_id_type=MESH
    )


def softmax_part(nh, s_top, s_low, dp_top, dp_low, d_top, d_low):
    half, early = HEAD, nh * HEAD
    keep = lax.broadcasted_iota(jnp.int32, (half, half), 0) <= lax.broadcasted_iota(
        jnp.int32, (half, half), 1
    )
    for j in range(2):
        rows = slice(j * half, (j + 1) * half)
        for h in range(nh):
            cols = slice(h * HEAD, (h + 1) * HEAD)
            back = slice(early + h * HEAD, early + (h + 1) * HEAD)
            a = jnp.where(keep, s_top[rows, cols], -1e30)
            m = jnp.max(a, axis=0, keepdims=True)
            e = jnp.exp2((a - m) * EXP2_SCALE)
            inv = 1.0 / jnp.sum(e, axis=0, keepdims=True)
            dp = dp_top[:, cols]
            center = jnp.sum(e * dp, axis=0, keepdims=True) * inv
            d_top[rows, cols] = (e * inv * (dp - center)).astype(BF16)
            a0 = s_top[rows, back]
            a1 = jnp.where(keep, s_low[rows, cols], -1e30)
            m = jnp.maximum(
                jnp.max(a0, axis=0, keepdims=True), jnp.max(a1, axis=0, keepdims=True)
            )
            e0 = jnp.exp2((a0 - m) * EXP2_SCALE)
            e1 = jnp.exp2((a1 - m) * EXP2_SCALE)
            inv = 1.0 / (jnp.sum(e0, axis=0, keepdims=True) + jnp.sum(e1, axis=0, keepdims=True))
            dp0 = dp_top[:, back]
            dp1 = dp_low[:, cols]
            center = (
                jnp.sum(e0 * dp0, axis=0, keepdims=True) + jnp.sum(e1 * dp1, axis=0, keepdims=True)
            ) * inv
            d_top[rows, back] = (e0 * inv * (dp0 - center)).astype(BF16)
            d_low[rows, cols] = (e1 * inv * (dp1 - center)).astype(BF16)


def step_kernel(
    nc, nt, donor_ref, heat_ref, w_ref, first_ref, second_ref, noise_ref, noise_b_ref,
    q_hbm, v_hbm, g_hbm, x_hbm,
    a_ref, b_ref,
    fa, fw, acc, base_ref, lr_ref, bt_ref,
    q_ref, v_ref, g_ref, x_ref, qt, qr, dp_top, dp_low, s_top, s_low, d_top, d_low,
    lgp, gb, rc, part, sib, ring, far_in, ybuf, kept_a, kept_b, piece, gbs, turn, lg,
    ssem, rsem, esem, loadsem, csem, ksem, sibsem, ringsem, ysem, gsem,
):
    at = Place(nc, nt)
    half, near, far = routes(at.nz)
    tokens = base_ref.shape[0]
    me = at.t
    rb = first_ref.shape[2]
    cb = second_ref.shape[1]
    gr = gb.shape[1]
    hg = gr // 2
    npb = nt // nc
    nh = q_ref.shape[1] // HEAD
    early = nh * HEAD
    two = 2 * RANK
    lo, hi = slice(0, HEAD), slice(HEAD, tokens)
    left, right = (at.c, at.tok(0, -1)), (at.c, at.tok(0, 1))
    across, sibling = (at.c, at.tok(1, 0)), (at.c, at.tok(0, 0, True))
    group = at.t // npb
    turned = [(group, at.c * npb + q) for q in range(npb)]
    is_me = [(group == at.c) & (at.c * npb + q == at.t) for q in range(npb)]

    wide = pl.ds(pl.multiple_of(at.c * early, HEAD), early)
    narrow = pl.ds(pl.multiple_of(at.c * HEAD, HEAD), HEAD)
    loads = [
        pltpu.make_async_copy(q_hbm.at[:, wide], q_ref, loadsem.at[0]),
        pltpu.make_async_copy(v_hbm.at[:, narrow], v_ref, loadsem.at[1]),
        pltpu.make_async_copy(g_hbm.at[:, wide], g_ref, loadsem.at[2]),
        pltpu.make_async_copy(x_hbm, x_ref, loadsem.at[3]),
    ]
    for cp in loads:
        cp.start()

    fa[me, pl.ds(0, rb), :] = jnp.concatenate([first_ref[0], first_ref[1]], axis=0).T.astype(BF16)
    fa[me, pl.ds(rb, cb), :] = jnp.concatenate([second_ref[0], second_ref[1]], axis=1).astype(BF16)
    fw[me] = w_ref[...]
    entry_barrier(
        [left, right, across, sibling] + [(at.chain(i), at.t) for i in range(1, nc)],
        [(dev, jnp.logical_not(is_own)) for dev, is_own in zip(turned, is_me)],
    )

    me_c = at.c

    def prepare():
        beside = []
        for j in range(2):
            heat = jnp.sqrt(jnp.full((1, rb), 2.0 * STRIDE_LENGTH * heat_ref[j], F32))
            kept_a[me_c, j * RANK : (j + 1) * RANK, :] = (
                (1.0 - STRIDE_LENGTH) * first_ref[j] + heat * noise_ref[j]
            )
            beside.append((1.0 - STRIDE_LENGTH) * second_ref[j] + heat[:, :RANK] * noise_b_ref[j])
        kept_b[me_c] = jnp.concatenate(beside, axis=1)
        for h in range(nh):
            cols = slice(h * HEAD, (h + 1) * HEAD)
            later = slice(early + h * HEAD, early + (h + 1) * HEAD)
            q_t = q_ref[:, cols].astype(F32).T.astype(BF16)
            qt[:, cols] = q_t[:, lo]
            qt[:, later] = q_t[:, hi]
            qr[cols] = q_ref[lo, cols]
            qr[later] = q_ref[hi, cols]
            top = dot(v_ref[lo], g_ref[:, cols], ((1,), (1,)))
            dp_top[:, cols] = top[:, lo]
            dp_top[:, later] = top[:, hi]
            dp_low[:, cols] = dot(v_ref[hi], g_ref[hi, cols], ((1,), (1,)))

    swaps = []
    for i in range(1, nc):
        dev = (at.chain(i), at.t)
        swaps.append(remote(kept_a.at[me_c], kept_a.at[me_c], ksem.at[0, 0, i], ksem.at[0, 1, i], dev))
        swaps.append(remote(kept_b.at[me_c], kept_b.at[me_c], ksem.at[1, 0, i], ksem.at[1, 1, i], dev))

    full = (fa, fw)
    sends = []

    def send(kind, b, dev):
        cp = remote(full[kind].at[b], full[kind].at[b], ssem.at[len(sends)], rsem.at[kind, b], dev)
        cp.start()
        sends.append(cp)

    def wait(kind, b):
        remote(full[kind].at[b], full[kind].at[b], ssem.at[0], rsem.at[kind, b], sibling).wait_recv()

    def products(kind, blocks):
        total = acc[kind]
        for b in blocks:
            cols = pl.ds(pl.multiple_of(b * rb, rb), rb)
            total += dot(x_ref[:, cols], full[kind][b, pl.ds(0, rb), :])
        acc[kind] = total

    groups = []
    for s in range(1, half + 1):
        group = []
        for way, onward, reach in ((-1, right, half), (1, left, half - 1)):
            if s <= reach:
                nxt = [onward] if s < reach else []
                if way * s in far or -way * s in far and s == half:
                    nxt = nxt + [across]
                group.append((0, way * s, nxt))
        if s == 1:
            group.append((1, 0, [right, left]))
        elif s - 1 <= near:
            for way, onward in ((-1, right), (1, left)):
                group.append((1, way * (s - 1), [onward] if s - 1 < near else []))
        groups.append(group)
    groups[-1] += [(1, d, []) for d in far if abs(d) < half]
    groups.append([(1, half, [])])

    def arrive(kind, group):
        blocks = []
        for other_yh, dz, nxt in group:
            b = at.tok(other_yh, dz)
            wait(kind, b)
            for dev in nxt:
                send(kind, b, dev)
            send(kind, b, sibling)
            blocks.append(b)
        return blocks

    def twins(kind, group):
        blocks = []
        for other_yh, dz, _ in group:
            b = at.tok(other_yh, dz, True)
            wait(kind, b)
            blocks.append(b)
        return blocks

    own = [(0, 0, [])]
    for kind in range(2):
        for dev in (right, left, across, sibling):
            send(kind, me, dev)
    acc[...] = jnp.zeros_like(acc)
    for cp in loads:
        cp.wait()
    prepare()
    last = len(groups)
    here = arrive(0, groups[0])
    products(0, here + [me] + twins(0, own))
    for g in range(1, last):
        here = arrive(0, groups[g])
        there = arrive(1, groups[g - 1]) if g < last - 1 else []
        products(0, here + twins(0, groups[g - 1]))
        if there:
            products(1, there)
    products(0, twins(0, groups[last - 1]))

    exchanges = []

    def exchange(src, dst, i, kind):
        cp = remote(src, dst, esem.at[kind, 0, i], esem.at[kind, 1, i], (at.chain(i), at.t))
        cp.start()
        exchanges.append(cp)

    lr_ref[at.c] = acc[0].astype(BF16)
    for i in range(1, nc):
        exchange(lr_ref.at[at.c], lr_ref.at[at.c], i, 1)
    for i in range(1, nc):
        exchange(fa.at[pl.ds(at.chain(i) * npb, npb), pl.ds(rb, cb), :], bt_ref.at[at.c], i, 0)
    for u in range(npb):
        bt_ref[at.c, u] = fa[at.c * npb + u, pl.ds(rb, cb), :]

    here = arrive(1, groups[last - 2])
    products(1, here + [me] + twins(1, own) + twins(1, groups[0]))
    here = arrive(1, groups[last - 1])
    for g in range(1, last):
        here += twins(1, groups[g])
    products(1, here)
    base_ref[...] = acc[1].astype(BF16)
    for cp in exchanges:
        cp.wait()
    for cp in sends:
        cp.wait_send()
    for cp in swaps:
        cp.start()

    lane = lax.broadcasted_iota(jnp.int32, (HEAD, HEAD), 1)

    def heads_of(i):
        return remote(
            lgp.at[at.chain(i)], rc.at[i], csem.at[0, i], csem.at[1, i], (at.chain(i), at.t)
        )

    def pair(p):
        keys, factors = [], []
        base = base_ref[...].astype(F32)
        for j in range(2):
            chain = donor_ref[2 * p + j]
            source = lax.shift_right_logical(chain, 1)
            odd = lax.bitwise_and(chain, 1)
            lr = lr_ref[source]
            bt = bt_ref[source].reshape(HEAD, HEAD).astype(F32)
            upper = (lane >= RANK).astype(jnp.int32)
            mine = jnp.where(upper == odd, bt, jnp.zeros_like(bt))
            keys.append((base + ADAPTER_SCALE * dot(lr, mine.astype(BF16), ((1,), (1,)))).astype(BF16))
            factors.append((odd == 1, lr, bt.T))
        s_top[...] = dot(jnp.concatenate([keys[0][lo], keys[1][lo]], axis=0), qt[...])
        s_low[...] = dot(jnp.concatenate([keys[0][hi], keys[1][hi]], axis=0), qt[:, early:])
        softmax_part(nh, s_top, s_low, dp_top, dp_low, d_top, d_low)
        kg_lo = (dot(d_top[...], qr[...]) * SCORE_SCALE).astype(BF16)
        kg_hi = (dot(d_low[...], qr[early:]) * SCORE_SCALE).astype(BF16)
        for j in range(2):
            odd, lr, b_rows = factors[j]
            here = slice(j * HEAD, (j + 1) * HEAD)
            kg = jnp.concatenate([kg_lo[here], kg_hi[here]], axis=0)
            b_mine = jnp.where(odd, b_rows[RANK:], b_rows[:RANK]).astype(BF16)
            lgp[p, j * RANK : (j + 1) * RANK, :] = (
                ADAPTER_SCALE * dot(b_mine, kg, ((1,), (1,)))
            ).astype(BF16)
            both = dot(lr, kg, ((0,), (0,)))
            grad_b = (ADAPTER_SCALE * jnp.where(odd, both[RANK:], both[:RANK])).astype(BF16)
            per = RANK // gr
            for u in range(per):
                gb[(2 * p + j) * per + u] = grad_b[u * gr : (u + 1) * gr]

    def peer_pair(i, carry):
        pair(at.chain(i))

        @pl.when(i < nc)
        def _():
            heads_of(i).start()

        return carry

    lax.fori_loop(1, nc + 1, peer_pair, 0)

    total = lgp[at.c].astype(F32)
    for i in range(1, nc):
        heads_of(i).wait_recv()
        total += rc[i].astype(F32)
    lg[...] = total.astype(BF16)

    order = [(1, d) for d in sorted(far, key=lambda d: -abs(d))]
    order += [(0, d) for d in sorted(far, key=lambda d: -abs(d))]
    for m in range(near, 0, -1):
        order += [(1, -m), (1, m), (0, -m), (0, m)]
    order += [(1, 0), (0, 0)]
    rank_of = {dest: i for i, dest in enumerate(order)}

    def block(b):
        cols = pl.ds(pl.multiple_of(b * rb, rb), rb)
        second = jnp.concatenate([gb[b, pl.ds(0, hg), :], gb[b, pl.ds(hg, hg), :]], axis=1)
        return dot(lg[...], x_ref[:, cols]), second

    def to_sibling(i, b):
        return remote(part.at[b], sib.at[i], sibsem.at[0, i], sibsem.at[1, i], sibling)

    sent = []
    for i, (other_yh, dz) in enumerate(order):
        b = at.tok(other_yh, dz, True)
        first, second = block(b)
        part[b, pl.ds(0, two), :] = first.astype(BF16)
        part[b, pl.ds(two, hg), :] = second
        cp = to_sibling(i, b)
        cp.start()
        sent.append(cp)

    def join(other_yh, dz):
        i = rank_of[other_yh, dz]
        b = at.tok(other_yh, dz)
        first, second = block(b)
        sent[i].wait_recv()
        part[b, pl.ds(0, two), :] = (first + sib[i, pl.ds(0, two), :].astype(F32)).astype(BF16)
        part[b, pl.ds(two, hg), :] = (
            second.astype(F32) + sib[i, pl.ds(two, hg), :].astype(F32)
        ).astype(BF16)
        return b

    def far_copy(dz):
        i = far.index(dz)
        return remote(
            part.at[at.tok(1, dz)], far_in.at[i], ysem.at[0, i], ysem.at[1, i], across
        )

    reach = {(0, 0): half, (0, 1): half - 1, (1, 0): near, (1, 1): near}

    def link(other_yh, way, s, b):
        return remote(
            part.at[b],
            ring.at[other_yh, way, s - 1],
            ringsem.at[0, other_yh, way, s - 1],
            ringsem.at[1, other_yh, way, s - 1],
            right if way == 0 else left,
        )

    def hop(other_yh, way, s):
        far_reach = reach[other_yh, way]
        dz = (far_reach + 1 - s) * (1 if way == 0 else -1)
        b = at.tok(other_yh, dz)
        adds = []
        if other_yh == 0 and dz in far:
            far_copy(dz).wait_recv()
            adds.append(far_in[far.index(dz)].astype(F32))
        if s > 1:
            link(other_yh, way, s - 1, b).wait_recv()
            adds.append(ring[other_yh, way, s - 2].astype(F32))
        if adds:
            value = part[b].astype(F32)
            for term in adds:
                value += term
            part[b] = value.astype(BF16)
        cp = link(other_yh, way, s, b)
        cp.start()
        sent.append(cp)

    def arrived(other_yh, b):
        value = part[b].astype(F32)
        for way in range(2):
            last = reach[other_yh, way]
            if last:
                link(other_yh, way, last, b).wait_recv()
                value += ring[other_yh, way, last - 1].astype(F32)
        return value

    for other_yh, dz in order:
        if other_yh == 1 and dz in far:
            join(1, dz)
            cp = far_copy(dz)
            cp.start()
            sent.append(cp)
    for other_yh, dz in order:
        if other_yh == 0 and dz in far:
            join(0, dz)
    for s in range(1, half + 1):
        m = near + 1 - s
        if m >= 1:
            join(1, m)
            hop(1, 0, s)
            join(1, -m)
            hop(1, 1, s)
        for way in range(2):
            if s <= reach[0, way]:
                dz = (reach[0, way] + 1 - s) * (1 if way == 0 else -1)
                if dz not in far:
                    join(0, dz)
                hop(0, way, s)
        if m == 0:
            b = join(1, 0)
            part[b] = arrived(1, b).astype(BF16)
            cross = remote(part.at[b], ybuf, ysem.at[0, len(far)], ysem.at[1, len(far)], across)
            cross.start()
    b = join(0, 0)
    value = arrived(0, b)
    cross.wait()
    value += ybuf[...].astype(F32)

    piece[pl.ds(0, hg), :] = value[two:, :HEAD]
    piece[pl.ds(hg, hg), :] = value[two:, HEAD:]
    slot = lax.rem(at.t, npb)
    for q in range(npb):
        cp = remote(piece, gbs.at[slot], gsem.at[0, q], gsem.at[1, slot], turned[q])
        local = pltpu.make_async_copy(piece, gbs.at[slot], gsem.at[1, slot])

        @pl.when(jnp.logical_not(is_me[q]))
        def _():
            cp.start()

        @pl.when(is_me[q])
        def _():
            local.start()

    for cp in swaps:
        cp.wait()
    kept_t = []
    for j in range(2):
        chain = donor_ref[2 * at.c + j]
        source = lax.shift_right_logical(chain, 1)
        odd = lax.bitwise_and(chain, 1) == 1
        whole = kept_a[source]
        rows = slice(j * RANK, (j + 1) * RANK)
        a_ref[j] = jnp.where(odd, whole[RANK:], whole[:RANK]) - STRIDE_LENGTH * value[rows]
        whole = kept_b[source]
        kept_t.append(jnp.where(odd, whole[:, RANK:], whole[:, :RANK]))
    for cp in sent:
        cp.wait_send()
    for i in range(1, nc):
        heads_of(i).wait_send()
    for q in range(npb):
        pltpu.make_async_copy(piece, gbs.at[q], gsem.at[1, q]).wait()
        cp = remote(piece, gbs.at[slot], gsem.at[0, q], gsem.at[1, slot], turned[q])

        @pl.when(jnp.logical_not(is_me[q]))
        def _():
            cp.wait_send()

    turn[...] = jnp.concatenate([gbs[q] for q in range(npb)], axis=0).T
    sums = turn[pl.ds(pl.multiple_of(slot * cb, cb), cb), :]
    for j in range(2):
        b_ref[j] = kept_t[j] - STRIDE_LENGTH * sums[:, j * RANK : (j + 1) * RANK]


def step(nc, nt, donor, heats, w, first, second, noise, noise_b, q, v, g, x):
    tokens = x.shape[0]
    rb, cb = first.shape[2], second.shape[1]
    nz = nt // 4
    half, near, far = routes(nz)
    nh = q.shape[1] // (nc * HEAD)
    gr = 2 * nc * RANK // nt
    rows = 2 * RANK + gr // 2
    vmem = pl.BlockSpec(memory_space=pltpu.VMEM)
    smem = pl.BlockSpec(memory_space=pltpu.SMEM)
    hbm = pl.BlockSpec(memory_space=pl.ANY)
    sem = pltpu.SemaphoreType.DMA
    return pl.pallas_call(
        functools.partial(step_kernel, nc, nt),
        out_shape=(
            jax.ShapeDtypeStruct(first.shape, F32),
            jax.ShapeDtypeStruct(second.shape, F32),
        ),
        in_specs=[smem] * 2 + [vmem] * 5 + [hbm] * 4,
        out_specs=(vmem,) * 2,
        scratch_shapes=[
            pltpu.VMEM((nt, rb + cb, HEAD), BF16),
            pltpu.VMEM((nt, rb, HEAD), BF16),
            pltpu.VMEM((2, tokens, HEAD), F32),
            pltpu.VMEM((tokens, HEAD), BF16),
            pltpu.VMEM((nc, tokens, HEAD), BF16),
            pltpu.VMEM((nc, nt // nc, cb, HEAD), BF16),
            pltpu.VMEM((tokens, nh * HEAD), BF16),
            pltpu.VMEM((tokens, HEAD), BF16),
            pltpu.VMEM((tokens, nh * HEAD), BF16),
            pltpu.VMEM(x.shape, BF16),
            pltpu.VMEM((HEAD, nh * tokens), BF16),
            pltpu.VMEM((nh * tokens, HEAD), BF16),
            pltpu.VMEM((HEAD, nh * tokens), F32),
            pltpu.VMEM((HEAD, nh * HEAD), F32),
            pltpu.VMEM((2 * HEAD, nh * tokens), F32),
            pltpu.VMEM((2 * HEAD, nh * HEAD), F32),
            pltpu.VMEM((2 * HEAD, nh * tokens), BF16),
            pltpu.VMEM((2 * HEAD, nh * HEAD), BF16),
            pltpu.VMEM((nc, 2 * RANK, tokens), BF16),
            pltpu.VMEM((nt, gr, HEAD), BF16),
            pltpu.VMEM((nc, 2 * RANK, tokens), BF16),
            pltpu.VMEM((nt, rows, rb), BF16),
            pltpu.VMEM((nt // 2, rows, rb), BF16),
            pltpu.VMEM((2, 2, half, rows, rb), BF16),
            pltpu.VMEM((len(far), rows, rb), BF16),
            pltpu.VMEM((rows, rb), BF16),
            pltpu.VMEM((nc, 2 * RANK, rb), F32),
            pltpu.VMEM((nc, cb, HEAD), F32),
            pltpu.VMEM((gr, HEAD), F32),
            pltpu.VMEM((nt // nc, gr, HEAD), F32),
            pltpu.VMEM((HEAD, HEAD), F32),
            pltpu.VMEM((2 * RANK, tokens), BF16),
            sem((4 * nt,)),
            sem((2, nt)),
            sem((2, 2, nc)),
            sem((4,)),
            sem((2, nc)),
            sem((2, 2, nc)),
            sem((2, nt // 2)),
            sem((2, 2, 2, half)),
            sem((2, len(far) + 1)),
            sem((2, nt // nc)),
        ],
        compiler_params=pltpu.CompilerParams(
            collective_id=0, has_side_effects=True, vmem_limit_bytes=VMEM_LIMIT
        ),
        name="step",
    )(donor, heats, w, first, second, noise, noise_b, q, v, g, x)


def per_device(nc, nt, x, q, v, g, w, first, second, noise, noise_b, heats, donor):
    first, second, noise, noise_b = (z.transpose(0, 2, 1) for z in (first, second, noise, noise_b))
    new = step(nc, nt, donor, heats, w, first, second, noise, noise_b, q, v, g, x)
    return tuple(z.transpose(0, 2, 1) for z in new)


def solution(mesh):
    return jax.shard_map(
        functools.partial(per_device, mesh.shape["chain"], mesh.shape["tok"]),
        mesh=mesh,
        in_specs=(
            P("tok", None),
            P("tok", None),
            P("tok", None),
            P("tok", None),
            P("tok", "chain"),
            P("chain", "tok", None),
            P("chain", None, "tok"),
            P("chain", "tok", None),
            P("chain", None, "tok"),
            P("chain"),
            P(),
        ),
        out_specs=(P("chain", "tok", None), P("chain", None, "tok")),
        check_vma=False,
    )
```

```python
import functools
import math

import jax
import jax.numpy as jnp
from jax import lax
from jax.experimental import pallas as pl
from jax.experimental.pallas import tpu as pltpu
from jax.sharding import PartitionSpec as P

MESH = pl.DeviceIdType.MESH
HEAD = 128
RANK = 64
MODEL_WIDTH = 8192
STRIDE_LENGTH = 0.2
ADAPTER_SCALE = 1.0 / math.sqrt(MODEL_WIDTH * RANK)
SCORE_SCALE = 1.0 / math.sqrt(HEAD)
EXP2_SCALE = SCORE_SCALE * math.log2(math.e)
VMEM_LIMIT = 56 * 1024 * 1024

F32 = jnp.float32
BF16 = jnp.bfloat16


def dot(a, b, dims=((1,), (0,))):
    return lax.dot_general(a, b, (dims, ((), ())), preferred_element_type=F32)


class Place:
    def __init__(self, nc, nt):
        self.nc, self.nt, self.nz = nc, nt, nt // 4
        self.c = lax.axis_index("chain")
        self.t = lax.axis_index("tok")
        self.k = lax.rem(self.t, 2)
        self.z = lax.rem(self.t // 2, self.nz)
        self.yh = self.t // (2 * self.nz)

    def tok(self, other_yh, dz, other_k=False):
        yh = 1 - self.yh if other_yh else self.yh
        k = 1 - self.k if other_k else self.k
        z = lax.rem(self.z + (dz + self.nz), self.nz)
        return (yh * self.nz + z) * 2 + k

    def chain(self, i):
        return lax.rem(self.c + i, self.nc)


def entry_barrier(devices):
    barrier = pltpu.get_barrier_semaphore()
    for dev in devices:
        pl.semaphore_signal(barrier, inc=1, device_id=dev, device_id_type=MESH)
    pl.semaphore_wait(barrier, len(devices))


def routes(nz):
    half, near = nz // 2, nz // 4
    far = [d for d in range(-(half - 1), half + 1) if abs(d) > near]
    return half, near, far


def remote(src, dst, ssem, rsem, dev):
    return pltpu.make_async_remote_copy(
        src_ref=src, dst_ref=dst, send_sem=ssem, recv_sem=rsem, device_id=dev, device_id_type=MESH
    )


def softmax_part(nh, s_top, s_low, dp_top, dp_low, d_top, d_low):
    half, early = HEAD, nh * HEAD
    keep = lax.broadcasted_iota(jnp.int32, (half, half), 0) <= lax.broadcasted_iota(
        jnp.int32, (half, half), 1
    )
    for j in range(2):
        rows = slice(j * half, (j + 1) * half)
        for h in range(nh):
            cols = slice(h * HEAD, (h + 1) * HEAD)
            back = slice(early + h * HEAD, early + (h + 1) * HEAD)
            a = jnp.where(keep, s_top[rows, cols], -1e30)
            m = jnp.max(a, axis=0, keepdims=True)
            e = jnp.exp2((a - m) * EXP2_SCALE)
            inv = 1.0 / jnp.sum(e, axis=0, keepdims=True)
            dp = dp_top[:, cols]
            center = jnp.sum(e * dp, axis=0, keepdims=True) * inv
            d_top[rows, cols] = (e * inv * (dp - center)).astype(BF16)
            a0 = s_top[rows, back]
            a1 = jnp.where(keep, s_low[rows, cols], -1e30)
            m = jnp.maximum(
                jnp.max(a0, axis=0, keepdims=True), jnp.max(a1, axis=0, keepdims=True)
            )
            e0 = jnp.exp2((a0 - m) * EXP2_SCALE)
            e1 = jnp.exp2((a1 - m) * EXP2_SCALE)
            inv = 1.0 / (jnp.sum(e0, axis=0, keepdims=True) + jnp.sum(e1, axis=0, keepdims=True))
            dp0 = dp_top[:, back]
            dp1 = dp_low[:, cols]
            center = (
                jnp.sum(e0 * dp0, axis=0, keepdims=True) + jnp.sum(e1 * dp1, axis=0, keepdims=True)
            ) * inv
            d_top[rows, back] = (e0 * inv * (dp0 - center)).astype(BF16)
            d_low[rows, cols] = (e1 * inv * (dp1 - center)).astype(BF16)


def step_kernel(
    nc, nt, donor_ref, heat_ref, w_ref, first_ref, second_ref, noise_ref, noise_b_ref,
    q_hbm, v_hbm, g_hbm, x_hbm,
    a_ref, b_ref,
    fa, fw, acc, base_ref, lr_ref, bt_ref,
    q_ref, v_ref, g_ref, x_ref, qt, qr, dp_top, dp_low, s_top, s_low, d_top, d_low,
    lgp, gbp, rc, gbc, part, sib, relay_in, near_in, far_in, ybuf, kept_a, kept_b, lg,
    ssem, rsem, esem, loadsem, csem, ksem, sibsem, relaysem, nearsem, ysem,
):
    at = Place(nc, nt)
    half, near, far = routes(at.nz)
    tokens = base_ref.shape[0]
    me = at.t
    rb = first_ref.shape[2]
    cb = second_ref.shape[1]
    hb = cb // 2
    npb = nt // nc
    nh = q_ref.shape[1] // HEAD
    early = nh * HEAD
    two = 2 * RANK
    lo, hi = slice(0, HEAD), slice(HEAD, tokens)
    left, right = (at.c, at.tok(0, -1)), (at.c, at.tok(0, 1))
    across, sibling = (at.c, at.tok(1, 0)), (at.c, at.tok(0, 0, True))
    wide = pl.ds(pl.multiple_of(at.c * early, HEAD), early)
    narrow = pl.ds(pl.multiple_of(at.c * HEAD, HEAD), HEAD)
    loads = [
        pltpu.make_async_copy(q_hbm.at[:, wide], q_ref, loadsem.at[0]),
        pltpu.make_async_copy(v_hbm.at[:, narrow], v_ref, loadsem.at[1]),
        pltpu.make_async_copy(g_hbm.at[:, wide], g_ref, loadsem.at[2]),
        pltpu.make_async_copy(x_hbm, x_ref, loadsem.at[3]),
    ]
    for cp in loads:
        cp.start()

    fa[me, pl.ds(0, rb), :] = jnp.concatenate([first_ref[0], first_ref[1]], axis=0).T.astype(BF16)
    fa[me, pl.ds(rb, cb), :] = jnp.concatenate([second_ref[0], second_ref[1]], axis=1).astype(BF16)
    fw[me] = w_ref[...]
    close = [d for d in range(-near, near + 1) if d != 0]
    entry_barrier(
        [across, sibling]
        + [(at.c, at.tok(0, d)) for d in close]
        + [(at.chain(i), at.t) for i in range(1, nc)]
    )

    me_c = at.c

    def prepare():
        beside = []
        for j in range(2):
            heat = jnp.sqrt(jnp.full((1, rb), 2.0 * STRIDE_LENGTH * heat_ref[j], F32))
            kept_a[me_c, j * RANK : (j + 1) * RANK, :] = (
                (1.0 - STRIDE_LENGTH) * first_ref[j] + heat * noise_ref[j]
            )
            beside.append((1.0 - STRIDE_LENGTH) * second_ref[j] + heat[:, :RANK] * noise_b_ref[j])
        kept_b[me_c] = jnp.concatenate(beside, axis=1)
        for h in range(nh):
            cols = slice(h * HEAD, (h + 1) * HEAD)
            later = slice(early + h * HEAD, early + (h + 1) * HEAD)
            q_t = q_ref[:, cols].astype(F32).T.astype(BF16)
            qt[:, cols] = q_t[:, lo]
            qt[:, later] = q_t[:, hi]
            qr[cols] = q_ref[lo, cols]
            qr[later] = q_ref[hi, cols]
            top = dot(v_ref[lo], g_ref[:, cols], ((1,), (1,)))
            dp_top[:, cols] = top[:, lo]
            dp_top[:, later] = top[:, hi]
            dp_low[:, cols] = dot(v_ref[hi], g_ref[hi, cols], ((1,), (1,)))

    swaps = []
    for i in range(1, nc):
        dev = (at.chain(i), at.t)
        swaps.append(remote(kept_a.at[me_c], kept_a.at[me_c], ksem.at[0, 0, i], ksem.at[0, 1, i], dev))
        swaps.append(remote(kept_b.at[me_c], kept_b.at[me_c], ksem.at[1, 0, i], ksem.at[1, 1, i], dev))

    full = (fa, fw)
    sends = []

    def send(kind, b, dev):
        cp = remote(full[kind].at[b], full[kind].at[b], ssem.at[len(sends)], rsem.at[kind, b], dev)
        cp.start()
        sends.append(cp)

    def wait(kind, b):
        remote(full[kind].at[b], full[kind].at[b], ssem.at[0], rsem.at[kind, b], sibling).wait_recv()

    def products(kind, blocks):
        total = acc[kind]
        for b in blocks:
            cols = pl.ds(pl.multiple_of(b * rb, rb), rb)
            total += dot(x_ref[:, cols], full[kind][b, pl.ds(0, rb), :])
        acc[kind] = total

    groups = []
    for s in range(1, half + 1):
        group = []
        for way, onward, reach in ((-1, right, half), (1, left, half - 1)):
            if s <= reach:
                nxt = [onward] if s < reach else []
                if way * s in far or -way * s in far and s == half:
                    nxt = nxt + [across]
                group.append((0, way * s, nxt))
        if s == 1:
            group.append((1, 0, [right, left]))
        elif s - 1 <= near:
            for way, onward in ((-1, right), (1, left)):
                group.append((1, way * (s - 1), [onward] if s - 1 < near else []))
        groups.append(group)
    groups[-1] += [(1, d, []) for d in far if abs(d) < half]
    groups.append([(1, half, [])])

    def arrive(kind, group):
        blocks = []
        for other_yh, dz, nxt in group:
            b = at.tok(other_yh, dz)
            wait(kind, b)
            for dev in nxt:
                send(kind, b, dev)
            send(kind, b, sibling)
            blocks.append(b)
        return blocks

    def twins(kind, group):
        blocks = []
        for other_yh, dz, _ in group:
            b = at.tok(other_yh, dz, True)
            wait(kind, b)
            blocks.append(b)
        return blocks

    own = [(0, 0, [])]
    for kind in range(2):
        for dev in (right, left, across, sibling):
            send(kind, me, dev)
    acc[...] = jnp.zeros_like(acc)
    for cp in loads:
        cp.wait()
    prepare()
    last = len(groups)
    here = arrive(0, groups[0])
    products(0, here + [me] + twins(0, own))
    for g in range(1, last):
        here = arrive(0, groups[g])
        there = arrive(1, groups[g - 1]) if g < last - 1 else []
        products(0, here + twins(0, groups[g - 1]))
        if there:
            products(1, there)
    products(0, twins(0, groups[last - 1]))

    exchanges = []

    def exchange(src, dst, i, kind):
        cp = remote(src, dst, esem.at[kind, 0, i], esem.at[kind, 1, i], (at.chain(i), at.t))
        cp.start()
        exchanges.append(cp)

    lr_ref[at.c] = acc[0].astype(BF16)
    for i in range(1, nc):
        exchange(lr_ref.at[at.c], lr_ref.at[at.c], i, 1)
    for i in range(1, nc):
        exchange(fa.at[pl.ds(at.chain(i) * npb, npb), pl.ds(rb, cb), :], bt_ref.at[at.c], i, 0)
    for u in range(npb):
        bt_ref[at.c, u] = fa[at.c * npb + u, pl.ds(rb, cb), :]

    here = arrive(1, groups[last - 2])
    products(1, here + [me] + twins(1, own) + twins(1, groups[0]))
    here = arrive(1, groups[last - 1])
    for g in range(1, last):
        here += twins(1, groups[g])
    products(1, here)
    base_ref[...] = acc[1].astype(BF16)
    for cp in exchanges:
        cp.wait()
    for cp in sends:
        cp.wait_send()
    for cp in swaps:
        cp.start()

    lane = lax.broadcasted_iota(jnp.int32, (HEAD, HEAD), 1)

    def heads_of(i):
        peer = at.chain(i)
        dev = (peer, at.t)
        return (
            remote(lgp.at[peer], rc.at[i], csem.at[0, 0, i], csem.at[0, 1, i], dev),
            remote(gbp.at[peer], gbc.at[at.c], csem.at[1, 0, i], csem.at[1, 1, i], dev),
        )

    def pair(p):
        keys, factors = [], []
        base = base_ref[...].astype(F32)
        for j in range(2):
            chain = donor_ref[2 * p + j]
            source = lax.shift_right_logical(chain, 1)
            odd = lax.bitwise_and(chain, 1)
            lr = lr_ref[source]
            bt = bt_ref[source].reshape(HEAD, HEAD).astype(F32)
            upper = (lane >= RANK).astype(jnp.int32)
            mine = jnp.where(upper == odd, bt, jnp.zeros_like(bt))
            keys.append((base + ADAPTER_SCALE * dot(lr, mine.astype(BF16), ((1,), (1,)))).astype(BF16))
            factors.append((odd == 1, lr, bt.T))
        s_top[...] = dot(jnp.concatenate([keys[0][lo], keys[1][lo]], axis=0), qt[...])
        s_low[...] = dot(jnp.concatenate([keys[0][hi], keys[1][hi]], axis=0), qt[:, early:])
        softmax_part(nh, s_top, s_low, dp_top, dp_low, d_top, d_low)
        grads_b = []
        kg_lo = (dot(d_top[...], qr[...]) * SCORE_SCALE).astype(BF16)
        kg_hi = (dot(d_low[...], qr[early:]) * SCORE_SCALE).astype(BF16)
        for j in range(2):
            odd, lr, b_rows = factors[j]
            here = slice(j * HEAD, (j + 1) * HEAD)
            kg = jnp.concatenate([kg_lo[here], kg_hi[here]], axis=0)
            b_mine = jnp.where(odd, b_rows[RANK:], b_rows[:RANK]).astype(BF16)
            lgp[p, j * RANK : (j + 1) * RANK, :] = (
                ADAPTER_SCALE * dot(b_mine, kg, ((1,), (1,)))
            ).astype(BF16)
            both = ADAPTER_SCALE * dot(kg, lr, ((0,), (0,)))
            grads_b.append(jnp.where(odd, both[:, RANK:], both[:, :RANK]))
        gbp[p] = jnp.concatenate(grads_b, axis=1).astype(BF16)

    def peer_pair(i, carry):
        pair(at.chain(i))

        @pl.when(i < nc)
        def _():
            for cp in heads_of(i):
                cp.start()

        return carry

    lax.fori_loop(1, nc + 1, peer_pair, 0)

    total = lgp[at.c].astype(F32)
    for i in range(1, nc):
        heads_of(i)[0].wait_recv()
        total += rc[i].astype(F32)
    lg[...] = total.astype(BF16)
    gbc[at.c] = gbp[at.c]
    for i in range(1, nc):
        heads_of(i)[1].wait_recv()

    far = sorted(far, key=lambda d: -abs(d))
    order = [(1, d) for d in far] + [(0, d) for d in far]
    order += [(1, d) for d in close] + [(0, d) for d in close] + [(1, 0), (0, 0)]

    def block(b):
        cols = pl.ds(pl.multiple_of(b * rb, rb), rb)
        start = pl.multiple_of(lax.rem(b, npb) * cb, cb)
        own_b = gbc.at[b // npb]
        second = jnp.concatenate(
            [own_b[pl.ds(start, hb), :], own_b[pl.ds(pl.multiple_of(start + hb, hb), hb), :]], axis=1
        )
        return dot(lg[...], x_ref[:, cols]), second

    sent = []
    passed = {}
    for i, (other_yh, dz) in enumerate(order):
        b = at.tok(other_yh, dz, True)
        first, second = block(b)
        part[b, pl.ds(0, two), :] = first.astype(BF16)
        part[b, pl.ds(two, hb), :] = second
        cp = remote(part.at[b], sib.at[i], sibsem.at[0, i], sibsem.at[1, i], sibling)
        cp.start()
        sent.append(cp)
        passed[other_yh, dz] = i, cp

    def join(other_yh, dz):
        i, cp = passed[other_yh, dz]
        b = at.tok(other_yh, dz)
        first, second = block(b)
        cp.wait_recv()
        part[b, pl.ds(0, two), :] = (first + sib[i, pl.ds(0, two), :].astype(F32)).astype(BF16)
        part[b, pl.ds(two, hb), :] = (
            second.astype(F32) + sib[i, pl.ds(two, hb), :].astype(F32)
        ).astype(BF16)
        return b

    def add(b, terms):
        value = part[b].astype(F32)
        for term in terms:
            value += term.astype(F32)
        return value

    def far_copy(dz):
        i = far.index(dz)
        return remote(part.at[at.tok(1, dz)], far_in.at[i], ysem.at[0, i], ysem.at[1, i], across)

    def relay(dz):
        i = far.index(dz)
        step = dz - near if dz > 0 else dz + near
        dev = (at.c, at.tok(0, step))
        return remote(part.at[at.tok(0, dz)], relay_in.at[i], relaysem.at[0, i], relaysem.at[1, i], dev)

    def direct(other_yh, dz):
        i = close.index(dz)
        return remote(
            part.at[at.tok(other_yh, dz)],
            near_in.at[other_yh, i],
            nearsem.at[0, other_yh, i],
            nearsem.at[1, other_yh, i],
            (at.c, at.tok(0, dz)),
        )

    def begin(cp):
        cp.start()
        sent.append(cp)
        return cp

    for dz in far:
        join(1, dz)
        begin(far_copy(dz))
    for dz in far:
        join(0, dz)
    for dz in far:
        b = at.tok(0, dz)
        far_copy(dz).wait_recv()
        part[b] = add(b, [far_in[far.index(dz)]]).astype(BF16)
        begin(relay(dz))
    for dz in close:
        join(1, dz)
        begin(direct(1, dz))
    for dz in close:
        join(0, dz)
        if abs(dz) < near:
            begin(direct(0, dz))
    join(1, 0)
    join(0, 0)
    for side in (1, -1):
        dz = side * near
        b = at.tok(0, dz)
        terms = []
        for d in far:
            if d * side > 0:
                relay(d).wait_recv()
                terms.append(relay_in[far.index(d)])
        part[b] = add(b, terms).astype(BF16)
        begin(direct(0, dz))

    def arrived(other_yh):
        for dz in close:
            direct(other_yh, dz).wait_recv()
        b = at.tok(other_yh, 0)
        return b, add(b, [near_in[other_yh, i] for i in range(len(close))])

    b, value = arrived(1)
    part[b] = value.astype(BF16)
    cross = remote(part.at[b], ybuf, ysem.at[0, len(far)], ysem.at[1, len(far)], across)
    cross.start()
    b, value = arrived(0)
    cross.wait()
    value += ybuf[...].astype(F32)
    sums_b = value[two:]

    for cp in swaps:
        cp.wait()
    for j in range(2):
        chain = donor_ref[2 * at.c + j]
        source = lax.shift_right_logical(chain, 1)
        odd = lax.bitwise_and(chain, 1) == 1
        whole = kept_a[source]
        rows = slice(j * RANK, (j + 1) * RANK)
        a_ref[j] = jnp.where(odd, whole[RANK:], whole[:RANK]) - STRIDE_LENGTH * value[rows]
        whole = kept_b[source]
        kept = jnp.where(odd, whole[:, RANK:], whole[:, :RANK])
        lanes = slice(j * RANK, (j + 1) * RANK)
        own_b = jnp.concatenate(
            [sums_b[:, lanes], sums_b[:, HEAD + j * RANK : HEAD + (j + 1) * RANK]], axis=0
        )
        b_ref[j] = kept - STRIDE_LENGTH * own_b
    for cp in sent:
        cp.wait_send()
    for i in range(1, nc):
        for cp in heads_of(i):
            cp.wait_send()


def step(nc, nt, donor, heats, w, first, second, noise, noise_b, q, v, g, x):
    tokens = x.shape[0]
    rb, cb = first.shape[2], second.shape[1]
    nz = nt // 4
    half, near, far = routes(nz)
    nh = q.shape[1] // (nc * HEAD)
    rows = 2 * RANK + cb // 2
    vmem = pl.BlockSpec(memory_space=pltpu.VMEM)
    smem = pl.BlockSpec(memory_space=pltpu.SMEM)
    hbm = pl.BlockSpec(memory_space=pl.ANY)
    sem = pltpu.SemaphoreType.DMA
    return pl.pallas_call(
        functools.partial(step_kernel, nc, nt),
        out_shape=(
            jax.ShapeDtypeStruct(first.shape, F32),
            jax.ShapeDtypeStruct(second.shape, F32),
        ),
        in_specs=[smem] * 2 + [vmem] * 5 + [hbm] * 4,
        out_specs=(vmem,) * 2,
        scratch_shapes=[
            pltpu.VMEM((nt, rb + cb, HEAD), BF16),
            pltpu.VMEM((nt, rb, HEAD), BF16),
            pltpu.VMEM((2, tokens, HEAD), F32),
            pltpu.VMEM((tokens, HEAD), BF16),
            pltpu.VMEM((nc, tokens, HEAD), BF16),
            pltpu.VMEM((nc, nt // nc, cb, HEAD), BF16),
            pltpu.VMEM((tokens, nh * HEAD), BF16),
            pltpu.VMEM((tokens, HEAD), BF16),
            pltpu.VMEM((tokens, nh * HEAD), BF16),
            pltpu.VMEM(x.shape, BF16),
            pltpu.VMEM((HEAD, nh * tokens), BF16),
            pltpu.VMEM((nh * tokens, HEAD), BF16),
            pltpu.VMEM((HEAD, nh * tokens), F32),
            pltpu.VMEM((HEAD, nh * HEAD), F32),
            pltpu.VMEM((2 * HEAD, nh * tokens), F32),
            pltpu.VMEM((2 * HEAD, nh * HEAD), F32),
            pltpu.VMEM((2 * HEAD, nh * tokens), BF16),
            pltpu.VMEM((2 * HEAD, nh * HEAD), BF16),
            pltpu.VMEM((nc, 2 * RANK, tokens), BF16),
            pltpu.VMEM((nc, HEAD, 2 * RANK), BF16),
            pltpu.VMEM((nc, 2 * RANK, tokens), BF16),
            pltpu.VMEM((nc, HEAD, 2 * RANK), BF16),
            pltpu.VMEM((nt, rows, rb), BF16),
            pltpu.VMEM((nt // 2, rows, rb), BF16),
            pltpu.VMEM((len(far), rows, rb), BF16),
            pltpu.VMEM((2, 2 * near, rows, rb), BF16),
            pltpu.VMEM((len(far), rows, rb), BF16),
            pltpu.VMEM((rows, rb), BF16),
            pltpu.VMEM((nc, 2 * RANK, rb), F32),
            pltpu.VMEM((nc, cb, HEAD), F32),
            pltpu.VMEM((2 * RANK, tokens), BF16),
            sem((4 * nt,)),
            sem((2, nt)),
            sem((2, 2, nc)),
            sem((4,)),
            sem((2, 2, nc)),
            sem((2, 2, nc)),
            sem((2, nt // 2)),
            sem((2, len(far))),
            sem((2, 2, 2 * near)),
            sem((2, len(far) + 1)),
        ],
        compiler_params=pltpu.CompilerParams(
            collective_id=0, has_side_effects=True, vmem_limit_bytes=VMEM_LIMIT
        ),
        name="step",
    )(donor, heats, w, first, second, noise, noise_b, q, v, g, x)


def settle_kernel(a_ref, b_ref, new_a_ref, new_b_ref):
    new_a_ref[...] = a_ref[...]
    new_b_ref[...] = b_ref[...]


def settle(a, b):
    vmem = pl.BlockSpec(memory_space=pltpu.VMEM)
    return pl.pallas_call(
        settle_kernel,
        out_shape=(jax.ShapeDtypeStruct(a.shape, F32), jax.ShapeDtypeStruct(b.shape, F32)),
        in_specs=[vmem] * 2,
        out_specs=(vmem,) * 2,
        name="settle",
    )(a, b)


def per_device(nc, nt, x, q, v, g, w, first, second, noise, noise_b, heats, donor):
    first, second, noise, noise_b = (z.transpose(0, 2, 1) for z in (first, second, noise, noise_b))
    new = settle(*step(nc, nt, donor, heats, w, first, second, noise, noise_b, q, v, g, x))
    return tuple(z.transpose(0, 2, 1) for z in new)


def solution(mesh):
    return jax.shard_map(
        functools.partial(per_device, mesh.shape["chain"], mesh.shape["tok"]),
        mesh=mesh,
        in_specs=(
            P("tok", None),
            P("tok", None),
            P("tok", None),
            P("tok", None),
            P("tok", "chain"),
            P("chain", "tok", None),
            P("chain", None, "tok"),
            P("chain", "tok", None),
            P("chain", None, "tok"),
            P("chain"),
            P(),
        ),
        out_specs=(P("chain", "tok", None), P("chain", None, "tok")),
        check_vma=False,
    )
```

```python
import functools
import math

import jax
import jax.numpy as jnp
from jax import lax
from jax.experimental import pallas as pl
from jax.experimental.pallas import tpu as pltpu
from jax.sharding import PartitionSpec as P

MESH = pl.DeviceIdType.MESH
HEAD = 128
RANK = 64
MODEL_WIDTH = 8192
STRIDE_LENGTH = 0.2
ADAPTER_SCALE = 1.0 / math.sqrt(MODEL_WIDTH * RANK)
SCORE_SCALE = 1.0 / math.sqrt(HEAD)
EXP2_SCALE = SCORE_SCALE * math.log2(math.e)
VMEM_LIMIT = 56 * 1024 * 1024

F32 = jnp.float32
BF16 = jnp.bfloat16


def dot(a, b, dims=((1,), (0,))):
    return lax.dot_general(a, b, (dims, ((), ())), preferred_element_type=F32)


class Place:
    def __init__(self, nc, nt):
        self.nc, self.nt, self.nz = nc, nt, nt // 4
        self.c = lax.axis_index("chain")
        self.t = lax.axis_index("tok")
        self.k = lax.rem(self.t, 2)
        self.z = lax.rem(self.t // 2, self.nz)
        self.yh = self.t // (2 * self.nz)

    def tok(self, other_yh, dz, other_k=False):
        yh = 1 - self.yh if other_yh else self.yh
        k = 1 - self.k if other_k else self.k
        z = lax.rem(self.z + (dz + self.nz), self.nz)
        return (yh * self.nz + z) * 2 + k

    def chain(self, i):
        return lax.rem(self.c + i, self.nc)


def entry_barrier(devices):
    barrier = pltpu.get_barrier_semaphore()
    for dev in devices:
        pl.semaphore_signal(barrier, inc=1, device_id=dev, device_id_type=MESH)
    pl.semaphore_wait(barrier, len(devices))


def routes(nz):
    half, near = nz // 2, nz // 4
    far = [d for d in range(-(half - 1), half + 1) if abs(d) > near]
    return half, near, far


def remote(src, dst, ssem, rsem, dev):
    return pltpu.make_async_remote_copy(
        src_ref=src, dst_ref=dst, send_sem=ssem, recv_sem=rsem, device_id=dev, device_id_type=MESH
    )


def softmax_part(nh, s_top, s_low, dp_top, dp_low, d_top, d_low):
    half, early = HEAD, nh * HEAD
    keep = lax.broadcasted_iota(jnp.int32, (half, half), 0) <= lax.broadcasted_iota(
        jnp.int32, (half, half), 1
    )
    for j in range(2):
        rows = slice(j * half, (j + 1) * half)
        for h in range(nh):
            cols = slice(h * HEAD, (h + 1) * HEAD)
            back = slice(early + h * HEAD, early + (h + 1) * HEAD)
            a = jnp.where(keep, s_top[rows, cols], -1e30)
            m = jnp.max(a, axis=0, keepdims=True)
            e = jnp.exp2((a - m) * EXP2_SCALE)
            inv = 1.0 / jnp.sum(e, axis=0, keepdims=True)
            dp = dp_top[:, cols]
            center = jnp.sum(e * dp, axis=0, keepdims=True) * inv
            d_top[rows, cols] = (e * inv * (dp - center)).astype(BF16)
            a0 = s_top[rows, back]
            a1 = jnp.where(keep, s_low[rows, cols], -1e30)
            m = jnp.maximum(
                jnp.max(a0, axis=0, keepdims=True), jnp.max(a1, axis=0, keepdims=True)
            )
            e0 = jnp.exp2((a0 - m) * EXP2_SCALE)
            e1 = jnp.exp2((a1 - m) * EXP2_SCALE)
            inv = 1.0 / (jnp.sum(e0, axis=0, keepdims=True) + jnp.sum(e1, axis=0, keepdims=True))
            dp0 = dp_top[:, back]
            dp1 = dp_low[:, cols]
            center = (
                jnp.sum(e0 * dp0, axis=0, keepdims=True) + jnp.sum(e1 * dp1, axis=0, keepdims=True)
            ) * inv
            d_top[rows, back] = (e0 * inv * (dp0 - center)).astype(BF16)
            d_low[rows, cols] = (e1 * inv * (dp1 - center)).astype(BF16)


def step_kernel(
    nc, nt, donor_ref, heat_ref, w_ref, first_ref, second_ref, noise_ref, noise_b_ref,
    q_hbm, v_hbm, g_hbm, x_hbm,
    a_ref, b_ref,
    fa, fw, acc, base_ref, lr_ref, bt_ref,
    q_ref, v_ref, g_ref, x_ref, qt, qr, dp_top, dp_low, s_top, s_low, d_top, d_low,
    lgp, gbp, rc, gbc, part, sib, relay_in, near_in, far_in, ybuf, kept_a, kept_b, lg,
    ssem, rsem, esem, bsem, loadsem, csem, ksem, sibsem, relaysem, nearsem, ysem,
):
    at = Place(nc, nt)
    half, near, far = routes(at.nz)
    tokens = base_ref.shape[0]
    me = at.t
    rb = first_ref.shape[2]
    cb = second_ref.shape[1]
    hb = cb // 2
    npb = nt // nc
    nh = q_ref.shape[1] // HEAD
    early = nh * HEAD
    two = 2 * RANK
    lo, hi = slice(0, HEAD), slice(HEAD, tokens)
    left, right = (at.c, at.tok(0, -1)), (at.c, at.tok(0, 1))
    across, sibling = (at.c, at.tok(1, 0)), (at.c, at.tok(0, 0, True))
    wide = pl.ds(pl.multiple_of(at.c * early, HEAD), early)
    narrow = pl.ds(pl.multiple_of(at.c * HEAD, HEAD), HEAD)
    loads = [
        pltpu.make_async_copy(q_hbm.at[:, wide], q_ref, loadsem.at[0]),
        pltpu.make_async_copy(v_hbm.at[:, narrow], v_ref, loadsem.at[1]),
        pltpu.make_async_copy(g_hbm.at[:, wide], g_ref, loadsem.at[2]),
        pltpu.make_async_copy(x_hbm, x_ref, loadsem.at[3]),
    ]
    for cp in loads:
        cp.start()

    fa[me, pl.ds(0, rb), :] = jnp.concatenate([first_ref[0], first_ref[1]], axis=0).T.astype(BF16)
    fa[me, pl.ds(rb, cb), :] = jnp.concatenate([second_ref[0], second_ref[1]], axis=1).astype(BF16)
    fw[me] = w_ref[...]
    close = [d for d in range(-near, near + 1) if d != 0]
    entry_barrier(
        [across, sibling]
        + [(at.c, at.tok(0, d)) for d in close]
        + [(at.chain(i), at.t) for i in range(1, nc)]
    )

    me_c = at.c

    def prepare():
        beside = []
        for j in range(2):
            heat = jnp.sqrt(jnp.full((1, rb), 2.0 * STRIDE_LENGTH * heat_ref[j], F32))
            kept_a[me_c, j * RANK : (j + 1) * RANK, :] = (
                (1.0 - STRIDE_LENGTH) * first_ref[j] + heat * noise_ref[j]
            ).astype(BF16)
            beside.append((1.0 - STRIDE_LENGTH) * second_ref[j] + heat[:, :RANK] * noise_b_ref[j])
        kept_b[me_c] = jnp.concatenate(beside, axis=1).astype(BF16)
        for h in range(nh):
            cols = slice(h * HEAD, (h + 1) * HEAD)
            later = slice(early + h * HEAD, early + (h + 1) * HEAD)
            q_t = q_ref[:, cols].astype(F32).T.astype(BF16)
            qt[:, cols] = q_t[:, lo]
            qt[:, later] = q_t[:, hi]
            qr[cols] = q_ref[lo, cols]
            qr[later] = q_ref[hi, cols]
            top = dot(v_ref[lo], g_ref[:, cols], ((1,), (1,)))
            dp_top[:, cols] = top[:, lo]
            dp_top[:, later] = top[:, hi]
            dp_low[:, cols] = dot(v_ref[hi], g_ref[hi, cols], ((1,), (1,)))

    swaps = []
    for i in range(1, nc):
        dev = (at.chain(i), at.t)
        swaps.append(remote(kept_a.at[me_c], kept_a.at[me_c], ksem.at[0, 0, i], ksem.at[0, 1, i], dev))
        swaps.append(remote(kept_b.at[me_c], kept_b.at[me_c], ksem.at[1, 0, i], ksem.at[1, 1, i], dev))

    full = (fa, fw)
    sends = []

    def send(kind, b, dev):
        cp = remote(full[kind].at[b], full[kind].at[b], ssem.at[len(sends)], rsem.at[kind, b], dev)
        cp.start()
        sends.append(cp)

    def wait(kind, b):
        remote(full[kind].at[b], full[kind].at[b], ssem.at[0], rsem.at[kind, b], sibling).wait_recv()

    def products(kind, blocks):
        total = acc[kind]
        for b in blocks:
            cols = pl.ds(pl.multiple_of(b * rb, rb), rb)
            total += dot(x_ref[:, cols], full[kind][b, pl.ds(0, rb), :])
        acc[kind] = total

    groups = []
    for s in range(1, half + 1):
        group = []
        for way, onward, reach in ((-1, right, half), (1, left, half - 1)):
            if s <= reach:
                nxt = [onward] if s < reach else []
                if way * s in far or -way * s in far and s == half:
                    nxt = nxt + [across]
                group.append((0, way * s, nxt))
        if s == 1:
            group.append((1, 0, [right, left]))
        elif s - 1 <= near:
            for way, onward in ((-1, right), (1, left)):
                group.append((1, way * (s - 1), [onward] if s - 1 < near else []))
        groups.append(group)
    groups[-1] += [(1, d, []) for d in far if abs(d) < half]
    groups.append([(1, half, [])])

    def arrive(kind, group):
        blocks = []
        for other_yh, dz, nxt in group:
            b = at.tok(other_yh, dz)
            wait(kind, b)
            for dev in nxt:
                send(kind, b, dev)
            send(kind, b, sibling)
            blocks.append(b)
        return blocks

    def twins(kind, group):
        blocks = []
        for other_yh, dz, _ in group:
            b = at.tok(other_yh, dz, True)
            wait(kind, b)
            blocks.append(b)
        return blocks

    def b_copy(b):
        return remote(
            fa.at[b, pl.ds(rb, cb), :],
            bt_ref.at[at.c, lax.rem(b, npb)],
            bsem.at[0, b],
            bsem.at[1, at.c * npb + lax.rem(b, npb)],
            (b // npb, at.t),
        )

    def pass_on(blocks):
        for b in blocks:

            @pl.when(b // npb == at.c)
            def _():
                bt_ref[at.c, lax.rem(b, npb)] = fa[b, pl.ds(rb, cb), :]

            @pl.when(b // npb != at.c)
            def _():
                b_copy(b).start()

    own = [(0, 0, [])]
    for dev in (right, left, across, sibling):
        send(0, me, dev)
    acc[...] = jnp.zeros_like(acc)
    for cp in loads:
        cp.wait()
    prepare()
    last = len(groups)
    here = arrive(0, groups[0])
    for cp in swaps:
        cp.start()
    own_twin = twins(0, own)
    pass_on([me] + own_twin + here)
    products(0, here + [me] + own_twin)
    for g in range(1, last):
        here = arrive(0, groups[g])
        if g == 1:
            for dev in (right, left, across, sibling):
                send(1, me, dev)
        there = arrive(1, groups[g - 2]) if g >= 2 else []
        here += twins(0, groups[g - 1])
        pass_on(here)
        products(0, here)
        if there:
            products(1, there)
    here = twins(0, groups[last - 1])
    pass_on(here)
    products(0, here)

    exchanges = []
    lr_ref[at.c] = acc[0].astype(BF16)
    for i in range(1, nc):
        cp = remote(
            lr_ref.at[at.c], lr_ref.at[at.c], esem.at[0, i], esem.at[1, i], (at.chain(i), at.t)
        )
        cp.start()
        exchanges.append(cp)

    pending = [me] + twins(1, own)
    for g in range(last - 2, last):
        here = arrive(1, groups[g])
        products(1, pending + here)
        pending = []
        for done in range(last - 2) if g == last - 2 else ():
            pending += twins(1, groups[done])
    for g in range(last - 2, last):
        pending += twins(1, groups[g])
    products(1, pending)
    base_ref[...] = acc[1].astype(BF16)
    for cp in exchanges:
        cp.wait()
    for i in range(1, nc):
        for u in range(npb):
            remote(
                bt_ref.at[0, u],
                bt_ref.at[0, u],
                bsem.at[0, 0],
                bsem.at[1, at.chain(i) * npb + u],
                sibling,
            ).wait_recv()
    for cp in sends:
        cp.wait_send()

    lane = lax.broadcasted_iota(jnp.int32, (HEAD, HEAD), 1)

    def heads_of(i):
        peer = at.chain(i)
        dev = (peer, at.t)
        return (
            remote(lgp.at[peer], rc.at[i], csem.at[0, 0, i], csem.at[0, 1, i], dev),
            remote(gbp.at[peer], gbc.at[at.c], csem.at[1, 0, i], csem.at[1, 1, i], dev),
        )

    def pair(p):
        keys, factors = [], []
        base = base_ref[...].astype(F32)
        for j in range(2):
            chain = donor_ref[2 * p + j]
            source = lax.shift_right_logical(chain, 1)
            odd = lax.bitwise_and(chain, 1)
            lr = lr_ref[source]
            bt = bt_ref[source].reshape(HEAD, HEAD).astype(F32)
            upper = (lane >= RANK).astype(jnp.int32)
            mine = jnp.where(upper == odd, bt, jnp.zeros_like(bt))
            keys.append((base + ADAPTER_SCALE * dot(lr, mine.astype(BF16), ((1,), (1,)))).astype(BF16))
            factors.append((odd == 1, lr, bt.T))
        s_top[...] = dot(jnp.concatenate([keys[0][lo], keys[1][lo]], axis=0), qt[...])
        s_low[...] = dot(jnp.concatenate([keys[0][hi], keys[1][hi]], axis=0), qt[:, early:])
        softmax_part(nh, s_top, s_low, dp_top, dp_low, d_top, d_low)
        grads_b = []
        kg_lo = (dot(d_top[...], qr[...]) * SCORE_SCALE).astype(BF16)
        kg_hi = (dot(d_low[...], qr[early:]) * SCORE_SCALE).astype(BF16)
        for j in range(2):
            odd, lr, b_rows = factors[j]
            here = slice(j * HEAD, (j + 1) * HEAD)
            kg = jnp.concatenate([kg_lo[here], kg_hi[here]], axis=0)
            b_mine = jnp.where(odd, b_rows[RANK:], b_rows[:RANK]).astype(BF16)
            lgp[p, j * RANK : (j + 1) * RANK, :] = (
                ADAPTER_SCALE * dot(b_mine, kg, ((1,), (1,)))
            ).astype(BF16)
            both = ADAPTER_SCALE * dot(kg, lr, ((0,), (0,)))
            grads_b.append(jnp.where(odd, both[:, RANK:], both[:, :RANK]))
        gbp[p] = jnp.concatenate(grads_b, axis=1).astype(BF16)

    def peer_pair(i, carry):
        pair(at.chain(i))

        @pl.when(i < nc)
        def _():
            for cp in heads_of(i):
                cp.start()

        return carry

    lax.fori_loop(1, nc + 1, peer_pair, 0)

    total = lgp[at.c].astype(F32)
    for i in range(1, nc):
        heads_of(i)[0].wait_recv()
        total += rc[i].astype(F32)
    lg[...] = total.astype(BF16)
    gbc[at.c] = gbp[at.c]
    for i in range(1, nc):
        heads_of(i)[1].wait_recv()

    far = sorted(far, key=lambda d: -abs(d))
    order = [(1, d) for d in far] + [(0, d) for d in far]
    order += [(1, d) for d in close] + [(0, d) for d in close] + [(1, 0), (0, 0)]

    def block(b):
        cols = pl.ds(pl.multiple_of(b * rb, rb), rb)
        start = pl.multiple_of(lax.rem(b, npb) * cb, cb)
        own_b = gbc.at[b // npb]
        second = jnp.concatenate(
            [own_b[pl.ds(start, hb), :], own_b[pl.ds(pl.multiple_of(start + hb, hb), hb), :]], axis=1
        )
        return dot(lg[...], x_ref[:, cols]), second

    sent = []
    passed = {}
    for i, (other_yh, dz) in enumerate(order):
        b = at.tok(other_yh, dz, True)
        first, second = block(b)
        part[b, pl.ds(0, two), :] = first.astype(BF16)
        part[b, pl.ds(two, hb), :] = second
        cp = remote(part.at[b], sib.at[i], sibsem.at[0, i], sibsem.at[1, i], sibling)
        cp.start()
        sent.append(cp)
        passed[other_yh, dz] = i, cp

    def join(other_yh, dz):
        i, cp = passed[other_yh, dz]
        b = at.tok(other_yh, dz)
        first, second = block(b)
        cp.wait_recv()
        part[b, pl.ds(0, two), :] = (first + sib[i, pl.ds(0, two), :].astype(F32)).astype(BF16)
        part[b, pl.ds(two, hb), :] = (
            second.astype(F32) + sib[i, pl.ds(two, hb), :].astype(F32)
        ).astype(BF16)
        return b

    def add(b, terms):
        value = part[b].astype(F32)
        for term in terms:
            value += term.astype(F32)
        return value

    def far_copy(dz):
        i = far.index(dz)
        return remote(part.at[at.tok(1, dz)], far_in.at[i], ysem.at[0, i], ysem.at[1, i], across)

    def relay(dz):
        i = far.index(dz)
        step = dz - near if dz > 0 else dz + near
        dev = (at.c, at.tok(0, step))
        return remote(part.at[at.tok(0, dz)], relay_in.at[i], relaysem.at[0, i], relaysem.at[1, i], dev)

    def direct(other_yh, dz):
        i = close.index(dz)
        return remote(
            part.at[at.tok(other_yh, dz)],
            near_in.at[other_yh, i],
            nearsem.at[0, other_yh, i],
            nearsem.at[1, other_yh, i],
            (at.c, at.tok(0, dz)),
        )

    def begin(cp):
        cp.start()
        sent.append(cp)
        return cp

    for dz in far:
        join(1, dz)
        begin(far_copy(dz))
    for dz in far:
        join(0, dz)
    for dz in far:
        b = at.tok(0, dz)
        far_copy(dz).wait_recv()
        part[b] = add(b, [far_in[far.index(dz)]]).astype(BF16)
        begin(relay(dz))
    for dz in close:
        join(1, dz)
        begin(direct(1, dz))
    for dz in close:
        join(0, dz)
        if abs(dz) < near:
            begin(direct(0, dz))
    join(1, 0)
    join(0, 0)
    for side in (1, -1):
        dz = side * near
        b = at.tok(0, dz)
        terms = []
        for d in far:
            if d * side > 0:
                relay(d).wait_recv()
                terms.append(relay_in[far.index(d)])
        part[b] = add(b, terms).astype(BF16)
        begin(direct(0, dz))

    def arrived(other_yh):
        for dz in close:
            direct(other_yh, dz).wait_recv()
        b = at.tok(other_yh, 0)
        return b, add(b, [near_in[other_yh, i] for i in range(len(close))])

    b, value = arrived(1)
    part[b] = value.astype(BF16)
    cross = remote(part.at[b], ybuf, ysem.at[0, len(far)], ysem.at[1, len(far)], across)
    cross.start()
    b, value = arrived(0)
    cross.wait()
    value += ybuf[...].astype(F32)
    sums_b = value[two:]

    for cp in swaps:
        cp.wait()
    for j in range(2):
        chain = donor_ref[2 * at.c + j]
        source = lax.shift_right_logical(chain, 1)
        odd = lax.bitwise_and(chain, 1) == 1
        whole = kept_a[source].astype(F32)
        rows = slice(j * RANK, (j + 1) * RANK)
        a_ref[j] = jnp.where(odd, whole[RANK:], whole[:RANK]) - STRIDE_LENGTH * value[rows]
        whole = kept_b[source].astype(F32)
        kept = jnp.where(odd, whole[:, RANK:], whole[:, :RANK])
        lanes = slice(j * RANK, (j + 1) * RANK)
        own_b = jnp.concatenate(
            [sums_b[:, lanes], sums_b[:, HEAD + j * RANK : HEAD + (j + 1) * RANK]], axis=0
        )
        b_ref[j] = kept - STRIDE_LENGTH * own_b
    for cp in sent:
        cp.wait_send()
    for i in range(1, nc):
        for cp in heads_of(i):
            cp.wait_send()

    def b_sent(b, carry):
        @pl.when(b // npb != at.c)
        def _():
            b_copy(b).wait_send()

        return carry

    lax.fori_loop(0, nt, b_sent, 0)


def step(nc, nt, donor, heats, w, first, second, noise, noise_b, q, v, g, x):
    tokens = x.shape[0]
    rb, cb = first.shape[2], second.shape[1]
    nz = nt // 4
    half, near, far = routes(nz)
    nh = q.shape[1] // (nc * HEAD)
    rows = 2 * RANK + cb // 2
    vmem = pl.BlockSpec(memory_space=pltpu.VMEM)
    smem = pl.BlockSpec(memory_space=pltpu.SMEM)
    hbm = pl.BlockSpec(memory_space=pl.ANY)
    sem = pltpu.SemaphoreType.DMA
    return pl.pallas_call(
        functools.partial(step_kernel, nc, nt),
        out_shape=(
            jax.ShapeDtypeStruct(first.shape, F32),
            jax.ShapeDtypeStruct(second.shape, F32),
        ),
        in_specs=[smem] * 2 + [vmem] * 5 + [hbm] * 4,
        out_specs=(vmem,) * 2,
        scratch_shapes=[
            pltpu.VMEM((nt, rb + cb, HEAD), BF16),
            pltpu.VMEM((nt, rb, HEAD), BF16),
            pltpu.VMEM((2, tokens, HEAD), F32),
            pltpu.VMEM((tokens, HEAD), BF16),
            pltpu.VMEM((nc, tokens, HEAD), BF16),
            pltpu.VMEM((nc, nt // nc, cb, HEAD), BF16),
            pltpu.VMEM((tokens, nh * HEAD), BF16),
            pltpu.VMEM((tokens, HEAD), BF16),
            pltpu.VMEM((tokens, nh * HEAD), BF16),
            pltpu.VMEM(x.shape, BF16),
            pltpu.VMEM((HEAD, nh * tokens), BF16),
            pltpu.VMEM((nh * tokens, HEAD), BF16),
            pltpu.VMEM((HEAD, nh * tokens), F32),
            pltpu.VMEM((HEAD, nh * HEAD), F32),
            pltpu.VMEM((2 * HEAD, nh * tokens), F32),
            pltpu.VMEM((2 * HEAD, nh * HEAD), F32),
            pltpu.VMEM((2 * HEAD, nh * tokens), BF16),
            pltpu.VMEM((2 * HEAD, nh * HEAD), BF16),
            pltpu.VMEM((nc, 2 * RANK, tokens), BF16),
            pltpu.VMEM((nc, HEAD, 2 * RANK), BF16),
            pltpu.VMEM((nc, 2 * RANK, tokens), BF16),
            pltpu.VMEM((nc, HEAD, 2 * RANK), BF16),
            pltpu.VMEM((nt, rows, rb), BF16),
            pltpu.VMEM((nt // 2, rows, rb), BF16),
            pltpu.VMEM((len(far), rows, rb), BF16),
            pltpu.VMEM((2, 2 * near, rows, rb), BF16),
            pltpu.VMEM((len(far), rows, rb), BF16),
            pltpu.VMEM((rows, rb), BF16),
            pltpu.VMEM((nc, 2 * RANK, rb), BF16),
            pltpu.VMEM((nc, cb, HEAD), BF16),
            pltpu.VMEM((2 * RANK, tokens), BF16),
            sem((4 * nt,)),
            sem((2, nt)),
            sem((2, nc)),
            sem((2, nt)),
            sem((4,)),
            sem((2, 2, nc)),
            sem((2, 2, nc)),
            sem((2, nt // 2)),
            sem((2, len(far))),
            sem((2, 2, 2 * near)),
            sem((2, len(far) + 1)),
        ],
        compiler_params=pltpu.CompilerParams(
            collective_id=0, has_side_effects=True, vmem_limit_bytes=VMEM_LIMIT
        ),
        name="step",
    )(donor, heats, w, first, second, noise, noise_b, q, v, g, x)


def settle_kernel(a_ref, b_ref, new_a_ref, new_b_ref):
    new_a_ref[...] = a_ref[...]
    new_b_ref[...] = b_ref[...]


def settle(a, b):
    vmem = pl.BlockSpec(memory_space=pltpu.VMEM)
    return pl.pallas_call(
        settle_kernel,
        out_shape=(jax.ShapeDtypeStruct(a.shape, F32), jax.ShapeDtypeStruct(b.shape, F32)),
        in_specs=[vmem] * 2,
        out_specs=(vmem,) * 2,
        name="settle",
    )(a, b)


def per_device(nc, nt, x, q, v, g, w, first, second, noise, noise_b, heats, donor):
    first, second, noise, noise_b = (z.transpose(0, 2, 1) for z in (first, second, noise, noise_b))
    new = settle(*step(nc, nt, donor, heats, w, first, second, noise, noise_b, q, v, g, x))
    return tuple(z.transpose(0, 2, 1) for z in new)


def solution(mesh):
    return jax.shard_map(
        functools.partial(per_device, mesh.shape["chain"], mesh.shape["tok"]),
        mesh=mesh,
        in_specs=(
            P("tok", None),
            P("tok", None),
            P("tok", None),
            P("tok", None),
            P("tok", "chain"),
            P("chain", "tok", None),
            P("chain", None, "tok"),
            P("chain", "tok", None),
            P("chain", None, "tok"),
            P("chain"),
            P(),
        ),
        out_specs=(P("chain", "tok", None), P("chain", None, "tok")),
        check_vma=False,
    )
```

```python
import functools
import math

import jax
import jax.numpy as jnp
from jax import lax
from jax.experimental import pallas as pl
from jax.experimental.pallas import tpu as pltpu
from jax.sharding import PartitionSpec as P

MESH = pl.DeviceIdType.MESH
HEAD = 128
RANK = 64
MODEL_WIDTH = 8192
STRIDE_LENGTH = 0.2
ADAPTER_SCALE = 1.0 / math.sqrt(MODEL_WIDTH * RANK)
SCORE_SCALE = 1.0 / math.sqrt(HEAD)
EXP2_SCALE = SCORE_SCALE * math.log2(math.e)
VMEM_LIMIT = 56 * 1024 * 1024

F32 = jnp.float32
BF16 = jnp.bfloat16


def dot(a, b, dims=((1,), (0,))):
    return lax.dot_general(a, b, (dims, ((), ())), preferred_element_type=F32)


class Place:
    def __init__(self, nc, nt):
        self.nc, self.nt, self.nz = nc, nt, nt // 4
        self.c = lax.axis_index("chain")
        self.t = lax.axis_index("tok")
        self.k = lax.rem(self.t, 2)
        self.z = lax.rem(self.t // 2, self.nz)
        self.yh = self.t // (2 * self.nz)

    def tok(self, other_yh, dz, other_k=False):
        yh = 1 - self.yh if other_yh else self.yh
        k = 1 - self.k if other_k else self.k
        z = lax.rem(self.z + (dz + self.nz), self.nz)
        return (yh * self.nz + z) * 2 + k

    def chain(self, i):
        return lax.rem(self.c + i, self.nc)


def entry_barrier(devices):
    barrier = pltpu.get_barrier_semaphore()
    for dev in devices:
        pl.semaphore_signal(barrier, inc=1, device_id=dev, device_id_type=MESH)
    pl.semaphore_wait(barrier, len(devices))


def routes(nz):
    half, near = nz // 2, nz // 4
    far = [d for d in range(-(half - 1), half + 1) if abs(d) > near]
    return half, near, far


def remote(src, dst, ssem, rsem, dev):
    return pltpu.make_async_remote_copy(
        src_ref=src, dst_ref=dst, send_sem=ssem, recv_sem=rsem, device_id=dev, device_id_type=MESH
    )


def softmax_part(nh, s_top, s_low, dp_top, dp_low, d_top, d_low):
    half, early = HEAD, nh * HEAD
    keep = lax.broadcasted_iota(jnp.int32, (half, half), 0) <= lax.broadcasted_iota(
        jnp.int32, (half, half), 1
    )
    for j in range(2):
        rows = slice(j * half, (j + 1) * half)
        for h in range(nh):
            cols = slice(h * HEAD, (h + 1) * HEAD)
            back = slice(early + h * HEAD, early + (h + 1) * HEAD)
            a = jnp.where(keep, s_top[rows, cols], -1e30)
            m = jnp.max(a, axis=0, keepdims=True)
            e = jnp.exp2((a - m) * EXP2_SCALE)
            inv = 1.0 / jnp.sum(e, axis=0, keepdims=True)
            dp = dp_top[:, cols]
            center = jnp.sum(e * dp, axis=0, keepdims=True) * inv
            d_top[rows, cols] = (e * inv * (dp - center)).astype(BF16)
            a0 = s_top[rows, back]
            a1 = jnp.where(keep, s_low[rows, cols], -1e30)
            m = jnp.maximum(
                jnp.max(a0, axis=0, keepdims=True), jnp.max(a1, axis=0, keepdims=True)
            )
            e0 = jnp.exp2((a0 - m) * EXP2_SCALE)
            e1 = jnp.exp2((a1 - m) * EXP2_SCALE)
            inv = 1.0 / (jnp.sum(e0, axis=0, keepdims=True) + jnp.sum(e1, axis=0, keepdims=True))
            dp0 = dp_top[:, back]
            dp1 = dp_low[:, cols]
            center = (
                jnp.sum(e0 * dp0, axis=0, keepdims=True) + jnp.sum(e1 * dp1, axis=0, keepdims=True)
            ) * inv
            d_top[rows, back] = (e0 * inv * (dp0 - center)).astype(BF16)
            d_low[rows, cols] = (e1 * inv * (dp1 - center)).astype(BF16)


def step_kernel(
    nc, nt, donor_ref, heat_ref, w_ref, first_ref, second_ref, noise_ref, noise_b_ref,
    q_hbm, v_hbm, g_hbm, x_hbm,
    a_ref, b_ref,
    fa, fw, acc, base_ref, lr_ref, bt_ref,
    q_ref, v_ref, g_ref, x_ref, qt, qr, dp_top, dp_low, s_top, s_low, d_top, d_low,
    lgp, gbp, rc, gbc, part, sib, relay_in, near_in, far_in, ybuf, kept_a, kept_b, lg,
    ssem, rsem, esem, bsem, loadsem, csem, ksem, sibsem, relaysem, nearsem, ysem,
):
    at = Place(nc, nt)
    half, near, far = routes(at.nz)
    tokens = base_ref.shape[0]
    me = at.t
    rb = first_ref.shape[2]
    cb = second_ref.shape[1]
    hb = cb // 2
    npb = nt // nc
    nh = q_ref.shape[1] // HEAD
    early = nh * HEAD
    two = 2 * RANK
    lo, hi = slice(0, HEAD), slice(HEAD, tokens)
    across, sibling = (at.c, at.tok(1, 0)), (at.c, at.tok(0, 0, True))
    wide = pl.ds(pl.multiple_of(at.c * early, HEAD), early)
    narrow = pl.ds(pl.multiple_of(at.c * HEAD, HEAD), HEAD)
    loads = [
        pltpu.make_async_copy(q_hbm.at[:, wide], q_ref, loadsem.at[0]),
        pltpu.make_async_copy(v_hbm.at[:, narrow], v_ref, loadsem.at[1]),
        pltpu.make_async_copy(g_hbm.at[:, wide], g_ref, loadsem.at[2]),
        pltpu.make_async_copy(x_hbm, x_ref, loadsem.at[3]),
    ]
    for cp in loads:
        cp.start()

    fa[me, pl.ds(0, rb), :] = jnp.concatenate([first_ref[0], first_ref[1]], axis=0).T.astype(BF16)
    fa[me, pl.ds(rb, cb), :] = jnp.concatenate([second_ref[0], second_ref[1]], axis=1).astype(BF16)
    fw[me] = w_ref[...]
    close = [d for d in range(-near, near + 1) if d != 0]
    entry_barrier(
        [across, sibling]
        + [(at.c, at.tok(0, d)) for d in close]
        + [(at.chain(i), at.t) for i in range(1, nc)]
    )

    me_c = at.c

    def prepare():
        beside = []
        for j in range(2):
            heat = jnp.sqrt(jnp.full((1, rb), 2.0 * STRIDE_LENGTH * heat_ref[j], F32))
            kept_a[me_c, j * RANK : (j + 1) * RANK, :] = (
                (1.0 - STRIDE_LENGTH) * first_ref[j] + heat * noise_ref[j]
            ).astype(BF16)
            beside.append((1.0 - STRIDE_LENGTH) * second_ref[j] + heat[:, :RANK] * noise_b_ref[j])
        kept_b[me_c] = jnp.concatenate(beside, axis=1).astype(BF16)
        for h in range(nh):
            cols = slice(h * HEAD, (h + 1) * HEAD)
            later = slice(early + h * HEAD, early + (h + 1) * HEAD)
            q_t = q_ref[:, cols].astype(F32).T.astype(BF16)
            qt[:, cols] = q_t[:, lo]
            qt[:, later] = q_t[:, hi]
            qr[cols] = q_ref[lo, cols]
            qr[later] = q_ref[hi, cols]
            top = dot(v_ref[lo], g_ref[:, cols], ((1,), (1,)))
            dp_top[:, cols] = top[:, lo]
            dp_top[:, later] = top[:, hi]
            dp_low[:, cols] = dot(v_ref[hi], g_ref[hi, cols], ((1,), (1,)))

    swaps = []
    for i in range(1, nc):
        dev = (at.chain(i), at.t)
        swaps.append(remote(kept_a.at[me_c], kept_a.at[me_c], ksem.at[0, 0, i], ksem.at[0, 1, i], dev))
        swaps.append(remote(kept_b.at[me_c], kept_b.at[me_c], ksem.at[1, 0, i], ksem.at[1, 1, i], dev))

    full = (fa, fw)
    sends = []

    def send(kind, b, dev):
        cp = remote(full[kind].at[b], full[kind].at[b], ssem.at[len(sends)], rsem.at[kind, b], dev)
        cp.start()
        sends.append(cp)

    def wait(kind, b):
        remote(full[kind].at[b], full[kind].at[b], ssem.at[0], rsem.at[kind, b], sibling).wait_recv()

    def products(kind, blocks):
        total = acc[kind]
        for b in blocks:
            cols = pl.ds(pl.multiple_of(b * rb, rb), rb)
            total += dot(x_ref[:, cols], full[kind][b, pl.ds(0, rb), :])
        acc[kind] = total

    beside_me = [(at.c, at.tok(0, d)) for d in close]

    def levels(kind):
        first = []
        for d in sorted(close, key=abs):
            nxt = [across] if kind == 0 else []
            for f in far:
                if f * d < 0 and abs(d) == near:
                    nxt = [(at.c, at.tok(0, f + d))] + nxt
            first.append((0, d, nxt))
        first.append((1, 0, beside_me if kind == 1 else []))
        second = [(0, -f, [across]) for f in far] + [(1, d, []) for d in close]
        return [first, second, [(1, -f, []) for f in far]]

    groups = (levels(0), levels(1))

    def arrive(kind, group):
        blocks = []
        for other_yh, dz, nxt in group:
            b = at.tok(other_yh, dz)
            wait(kind, b)
            for dev in nxt:
                send(kind, b, dev)
            send(kind, b, sibling)
            blocks.append(b)
        return blocks

    def twins(kind, group):
        blocks = []
        for other_yh, dz, _ in group:
            b = at.tok(other_yh, dz, True)
            wait(kind, b)
            blocks.append(b)
        return blocks

    def b_copy(b):
        return remote(
            fa.at[b, pl.ds(rb, cb), :],
            bt_ref.at[at.c, lax.rem(b, npb)],
            bsem.at[0, b],
            bsem.at[1, at.c * npb + lax.rem(b, npb)],
            (b // npb, at.t),
        )

    def pass_on(blocks):
        for b in blocks:

            @pl.when(b // npb == at.c)
            def _():
                bt_ref[at.c, lax.rem(b, npb)] = fa[b, pl.ds(rb, cb), :]

            @pl.when(b // npb != at.c)
            def _():
                b_copy(b).start()

    own = [(0, 0, [])]
    for dev in beside_me + [across, sibling]:
        send(0, me, dev)
    acc[...] = jnp.zeros_like(acc)
    for cp in loads:
        cp.wait()
    prepare()
    here = arrive(0, groups[0][0])
    for dev in beside_me + [across, sibling]:
        send(1, me, dev)
    here += [me] + twins(0, own)
    pass_on(here)
    products(0, here)
    here = arrive(0, groups[0][1])
    there = arrive(1, groups[1][0])
    here += twins(0, groups[0][0])
    pass_on(here)
    products(0, here)
    here = arrive(0, groups[0][2]) + twins(0, groups[0][1]) + twins(0, groups[0][2])
    pass_on(here)
    products(0, here)

    exchanges = []
    lr_ref[at.c] = acc[0].astype(BF16)
    for i in range(1, nc):
        cp = remote(
            lr_ref.at[at.c], lr_ref.at[at.c], esem.at[0, i], esem.at[1, i], (at.chain(i), at.t)
        )
        cp.start()
        exchanges.append(cp)

    here = arrive(1, groups[1][1])
    products(1, there + here + [me] + twins(1, own) + twins(1, groups[1][0]))
    here = arrive(1, groups[1][2])
    products(1, here + twins(1, groups[1][1]) + twins(1, groups[1][2]))
    base_ref[...] = acc[1].astype(BF16)
    for cp in exchanges:
        cp.wait()
    for i in range(1, nc):
        for u in range(npb):
            remote(
                bt_ref.at[0, u],
                bt_ref.at[0, u],
                bsem.at[0, 0],
                bsem.at[1, at.chain(i) * npb + u],
                sibling,
            ).wait_recv()
    for cp in sends:
        cp.wait_send()

    for cp in swaps:
        cp.start()

    lane = lax.broadcasted_iota(jnp.int32, (HEAD, HEAD), 1)

    def heads_of(i):
        peer = at.chain(i)
        dev = (peer, at.t)
        return (
            remote(lgp.at[peer], rc.at[i], csem.at[0, 0, i], csem.at[0, 1, i], dev),
            remote(gbp.at[peer], gbc.at[at.c], csem.at[1, 0, i], csem.at[1, 1, i], dev),
        )

    def pair(p):
        keys, factors = [], []
        base = base_ref[...].astype(F32)
        for j in range(2):
            chain = donor_ref[2 * p + j]
            source = lax.shift_right_logical(chain, 1)
            odd = lax.bitwise_and(chain, 1)
            lr = lr_ref[source]
            bt = bt_ref[source].reshape(HEAD, HEAD).astype(F32)
            upper = (lane >= RANK).astype(jnp.int32)
            mine = jnp.where(upper == odd, bt, jnp.zeros_like(bt))
            keys.append((base + ADAPTER_SCALE * dot(lr, mine.astype(BF16), ((1,), (1,)))).astype(BF16))
            factors.append((odd == 1, lr, bt.T))
        s_top[...] = dot(jnp.concatenate([keys[0][lo], keys[1][lo]], axis=0), qt[...])
        s_low[...] = dot(jnp.concatenate([keys[0][hi], keys[1][hi]], axis=0), qt[:, early:])
        softmax_part(nh, s_top, s_low, dp_top, dp_low, d_top, d_low)
        grads_b = []
        kg_lo = (dot(d_top[...], qr[...]) * SCORE_SCALE).astype(BF16)
        kg_hi = (dot(d_low[...], qr[early:]) * SCORE_SCALE).astype(BF16)
        for j in range(2):
            odd, lr, b_rows = factors[j]
            here = slice(j * HEAD, (j + 1) * HEAD)
            kg = jnp.concatenate([kg_lo[here], kg_hi[here]], axis=0)
            b_mine = jnp.where(odd, b_rows[RANK:], b_rows[:RANK]).astype(BF16)
            lgp[p, j * RANK : (j + 1) * RANK, :] = (
                ADAPTER_SCALE * dot(b_mine, kg, ((1,), (1,)))
            ).astype(BF16)
            both = ADAPTER_SCALE * dot(kg, lr, ((0,), (0,)))
            grads_b.append(jnp.where(odd, both[:, RANK:], both[:, :RANK]))
        gbp[p] = jnp.concatenate(grads_b, axis=1).astype(BF16)

    def peer_pair(i, carry):
        pair(at.chain(i))

        @pl.when(i < nc)
        def _():
            for cp in heads_of(i):
                cp.start()

        return carry

    lax.fori_loop(1, nc + 1, peer_pair, 0)

    total = lgp[at.c].astype(F32)
    for i in range(1, nc):
        heads_of(i)[0].wait_recv()
        total += rc[i].astype(F32)
    lg[...] = total.astype(BF16)
    gbc[at.c] = gbp[at.c]
    for i in range(1, nc):
        heads_of(i)[1].wait_recv()

    far = sorted(far, key=lambda d: -abs(d))
    order = [(1, d) for d in far] + [(0, d) for d in far]
    order += [(1, d) for d in close] + [(0, d) for d in close] + [(1, 0), (0, 0)]

    def block(b):
        cols = pl.ds(pl.multiple_of(b * rb, rb), rb)
        start = pl.multiple_of(lax.rem(b, npb) * cb, cb)
        own_b = gbc.at[b // npb]
        second = jnp.concatenate(
            [own_b[pl.ds(start, hb), :], own_b[pl.ds(pl.multiple_of(start + hb, hb), hb), :]], axis=1
        )
        return dot(lg[...], x_ref[:, cols]), second

    sent = []
    passed = {}
    for i, (other_yh, dz) in enumerate(order):
        b = at.tok(other_yh, dz, True)
        first, second = block(b)
        part[b, pl.ds(0, two), :] = first.astype(BF16)
        part[b, pl.ds(two, hb), :] = second
        cp = remote(part.at[b], sib.at[i], sibsem.at[0, i], sibsem.at[1, i], sibling)
        cp.start()
        sent.append(cp)
        passed[other_yh, dz] = i, cp

    def join(other_yh, dz):
        i, cp = passed[other_yh, dz]
        b = at.tok(other_yh, dz)
        first, second = block(b)
        cp.wait_recv()
        part[b, pl.ds(0, two), :] = (first + sib[i, pl.ds(0, two), :].astype(F32)).astype(BF16)
        part[b, pl.ds(two, hb), :] = (
            second.astype(F32) + sib[i, pl.ds(two, hb), :].astype(F32)
        ).astype(BF16)
        return b

    def add(b, terms):
        value = part[b].astype(F32)
        for term in terms:
            value += term.astype(F32)
        return value

    def far_copy(dz):
        i = far.index(dz)
        return remote(part.at[at.tok(1, dz)], far_in.at[i], ysem.at[0, i], ysem.at[1, i], across)

    def relay(dz):
        i = far.index(dz)
        step = dz - near if dz > 0 else dz + near
        dev = (at.c, at.tok(0, step))
        return remote(part.at[at.tok(0, dz)], relay_in.at[i], relaysem.at[0, i], relaysem.at[1, i], dev)

    def direct(other_yh, dz):
        i = close.index(dz)
        return remote(
            part.at[at.tok(other_yh, dz)],
            near_in.at[other_yh, i],
            nearsem.at[0, other_yh, i],
            nearsem.at[1, other_yh, i],
            (at.c, at.tok(0, dz)),
        )

    def begin(cp):
        cp.start()
        sent.append(cp)
        return cp

    for dz in far:
        join(1, dz)
        begin(far_copy(dz))
    for dz in far:
        join(0, dz)
    for dz in far:
        b = at.tok(0, dz)
        far_copy(dz).wait_recv()
        part[b] = add(b, [far_in[far.index(dz)]]).astype(BF16)
        begin(relay(dz))
    for dz in close:
        join(1, dz)
        begin(direct(1, dz))
    for dz in close:
        join(0, dz)
        if abs(dz) < near:
            begin(direct(0, dz))
    join(1, 0)
    join(0, 0)
    for side in (1, -1):
        dz = side * near
        b = at.tok(0, dz)
        terms = []
        for d in far:
            if d * side > 0:
                relay(d).wait_recv()
                terms.append(relay_in[far.index(d)])
        part[b] = add(b, terms).astype(BF16)
        begin(direct(0, dz))

    def arrived(other_yh):
        for dz in close:
            direct(other_yh, dz).wait_recv()
        b = at.tok(other_yh, 0)
        return b, add(b, [near_in[other_yh, i] for i in range(len(close))])

    b, value = arrived(1)
    part[b] = value.astype(BF16)
    cross = remote(part.at[b], ybuf, ysem.at[0, len(far)], ysem.at[1, len(far)], across)
    cross.start()
    b, value = arrived(0)
    cross.wait()
    value += ybuf[...].astype(F32)
    sums_b = value[two:]

    for cp in swaps:
        cp.wait()
    for j in range(2):
        chain = donor_ref[2 * at.c + j]
        source = lax.shift_right_logical(chain, 1)
        odd = lax.bitwise_and(chain, 1) == 1
        whole = kept_a[source].astype(F32)
        rows = slice(j * RANK, (j + 1) * RANK)
        a_ref[j] = jnp.where(odd, whole[RANK:], whole[:RANK]) - STRIDE_LENGTH * value[rows]
        whole = kept_b[source].astype(F32)
        kept = jnp.where(odd, whole[:, RANK:], whole[:, :RANK])
        lanes = slice(j * RANK, (j + 1) * RANK)
        own_b = jnp.concatenate(
            [sums_b[:, lanes], sums_b[:, HEAD + j * RANK : HEAD + (j + 1) * RANK]], axis=0
        )
        b_ref[j] = kept - STRIDE_LENGTH * own_b
    for cp in sent:
        cp.wait_send()
    for i in range(1, nc):
        for cp in heads_of(i):
            cp.wait_send()

    def b_sent(b, carry):
        @pl.when(b // npb != at.c)
        def _():
            b_copy(b).wait_send()

        return carry

    lax.fori_loop(0, nt, b_sent, 0)


def step(nc, nt, donor, heats, w, first, second, noise, noise_b, q, v, g, x):
    tokens = x.shape[0]
    rb, cb = first.shape[2], second.shape[1]
    nz = nt // 4
    half, near, far = routes(nz)
    nh = q.shape[1] // (nc * HEAD)
    rows = 2 * RANK + cb // 2
    vmem = pl.BlockSpec(memory_space=pltpu.VMEM)
    smem = pl.BlockSpec(memory_space=pltpu.SMEM)
    hbm = pl.BlockSpec(memory_space=pl.ANY)
    sem = pltpu.SemaphoreType.DMA
    return pl.pallas_call(
        functools.partial(step_kernel, nc, nt),
        out_shape=(
            jax.ShapeDtypeStruct(first.shape, F32),
            jax.ShapeDtypeStruct(second.shape, F32),
        ),
        in_specs=[smem] * 2 + [vmem] * 5 + [hbm] * 4,
        out_specs=(vmem,) * 2,
        scratch_shapes=[
            pltpu.VMEM((nt, rb + cb, HEAD), BF16),
            pltpu.VMEM((nt, rb, HEAD), BF16),
            pltpu.VMEM((2, tokens, HEAD), F32),
            pltpu.VMEM((tokens, HEAD), BF16),
            pltpu.VMEM((nc, tokens, HEAD), BF16),
            pltpu.VMEM((nc, nt // nc, cb, HEAD), BF16),
            pltpu.VMEM((tokens, nh * HEAD), BF16),
            pltpu.VMEM((tokens, HEAD), BF16),
            pltpu.VMEM((tokens, nh * HEAD), BF16),
            pltpu.VMEM(x.shape, BF16),
            pltpu.VMEM((HEAD, nh * tokens), BF16),
            pltpu.VMEM((nh * tokens, HEAD), BF16),
            pltpu.VMEM((HEAD, nh * tokens), F32),
            pltpu.VMEM((HEAD, nh * HEAD), F32),
            pltpu.VMEM((2 * HEAD, nh * tokens), F32),
            pltpu.VMEM((2 * HEAD, nh * HEAD), F32),
            pltpu.VMEM((2 * HEAD, nh * tokens), BF16),
            pltpu.VMEM((2 * HEAD, nh * HEAD), BF16),
            pltpu.VMEM((nc, 2 * RANK, tokens), BF16),
            pltpu.VMEM((nc, HEAD, 2 * RANK), BF16),
            pltpu.VMEM((nc, 2 * RANK, tokens), BF16),
            pltpu.VMEM((nc, HEAD, 2 * RANK), BF16),
            pltpu.VMEM((nt, rows, rb), BF16),
            pltpu.VMEM((nt // 2, rows, rb), BF16),
            pltpu.VMEM((len(far), rows, rb), BF16),
            pltpu.VMEM((2, 2 * near, rows, rb), BF16),
            pltpu.VMEM((len(far), rows, rb), BF16),
            pltpu.VMEM((rows, rb), BF16),
            pltpu.VMEM((nc, 2 * RANK, rb), BF16),
            pltpu.VMEM((nc, cb, HEAD), BF16),
            pltpu.VMEM((2 * RANK, tokens), BF16),
            sem((4 * nt,)),
            sem((2, nt)),
            sem((2, nc)),
            sem((2, nt)),
            sem((4,)),
            sem((2, 2, nc)),
            sem((2, 2, nc)),
            sem((2, nt // 2)),
            sem((2, len(far))),
            sem((2, 2, 2 * near)),
            sem((2, len(far) + 1)),
        ],
        compiler_params=pltpu.CompilerParams(
            collective_id=0, has_side_effects=True, vmem_limit_bytes=VMEM_LIMIT
        ),
        name="step",
    )(donor, heats, w, first, second, noise, noise_b, q, v, g, x)


def settle_kernel(a_ref, b_ref, new_a_ref, new_b_ref):
    new_a_ref[...] = a_ref[...]
    new_b_ref[...] = b_ref[...]


def settle(a, b):
    vmem = pl.BlockSpec(memory_space=pltpu.VMEM)
    return pl.pallas_call(
        settle_kernel,
        out_shape=(jax.ShapeDtypeStruct(a.shape, F32), jax.ShapeDtypeStruct(b.shape, F32)),
        in_specs=[vmem] * 2,
        out_specs=(vmem,) * 2,
        name="settle",
    )(a, b)


def per_device(nc, nt, x, q, v, g, w, first, second, noise, noise_b, heats, donor):
    first, second, noise, noise_b = (z.transpose(0, 2, 1) for z in (first, second, noise, noise_b))
    new = settle(*step(nc, nt, donor, heats, w, first, second, noise, noise_b, q, v, g, x))
    return tuple(z.transpose(0, 2, 1) for z in new)


def solution(mesh):
    return jax.shard_map(
        functools.partial(per_device, mesh.shape["chain"], mesh.shape["tok"]),
        mesh=mesh,
        in_specs=(
            P("tok", None),
            P("tok", None),
            P("tok", None),
            P("tok", None),
            P("tok", "chain"),
            P("chain", "tok", None),
            P("chain", None, "tok"),
            P("chain", "tok", None),
            P("chain", None, "tok"),
            P("chain"),
            P(),
        ),
        out_specs=(P("chain", "tok", None), P("chain", None, "tok")),
        check_vma=False,
    )
```

```python
import functools
import math

import jax
import jax.numpy as jnp
from jax import lax
from jax.experimental import pallas as pl
from jax.experimental.pallas import tpu as pltpu
from jax.sharding import PartitionSpec as P

MESH = pl.DeviceIdType.MESH
HEAD = 128
RANK = 64
MODEL_WIDTH = 8192
STRIDE_LENGTH = 0.2
ADAPTER_SCALE = 1.0 / math.sqrt(MODEL_WIDTH * RANK)
SCORE_SCALE = 1.0 / math.sqrt(HEAD)
EXP2_SCALE = SCORE_SCALE * math.log2(math.e)
VMEM_LIMIT = 56 * 1024 * 1024

F32 = jnp.float32
BF16 = jnp.bfloat16


def dot(a, b, dims=((1,), (0,))):
    return lax.dot_general(a, b, (dims, ((), ())), preferred_element_type=F32)


class Place:
    def __init__(self, nc, nt):
        self.nc, self.nt, self.nz = nc, nt, nt // 4
        self.c = lax.axis_index("chain")
        self.t = lax.axis_index("tok")
        self.k = lax.rem(self.t, 2)
        self.z = lax.rem(self.t // 2, self.nz)
        self.yh = self.t // (2 * self.nz)

    def tok(self, other_yh, dz, other_k=False):
        yh = 1 - self.yh if other_yh else self.yh
        k = 1 - self.k if other_k else self.k
        z = lax.rem(self.z + (dz + self.nz), self.nz)
        return (yh * self.nz + z) * 2 + k

    def chain(self, i):
        return lax.rem(self.c + i, self.nc)


def entry_barrier(devices):
    barrier = pltpu.get_barrier_semaphore()
    for dev in devices:
        pl.semaphore_signal(barrier, inc=1, device_id=dev, device_id_type=MESH)
    pl.semaphore_wait(barrier, len(devices))


def routes(nz):
    half, near = nz // 2, nz // 4
    far = [d for d in range(-(half - 1), half + 1) if abs(d) > near]
    return half, near, far


def remote(src, dst, ssem, rsem, dev):
    return pltpu.make_async_remote_copy(
        src_ref=src, dst_ref=dst, send_sem=ssem, recv_sem=rsem, device_id=dev, device_id_type=MESH
    )


def softmax_part(nh, s_top, s_low, dp_top, dp_low, d_top, d_low):
    half, early = HEAD, nh * HEAD
    keep = lax.broadcasted_iota(jnp.int32, (half, half), 0) <= lax.broadcasted_iota(
        jnp.int32, (half, half), 1
    )
    for j in range(2):
        rows = slice(j * half, (j + 1) * half)
        for h in range(nh):
            cols = slice(h * HEAD, (h + 1) * HEAD)
            back = slice(early + h * HEAD, early + (h + 1) * HEAD)
            a = jnp.where(keep, s_top[rows, cols], -1e30)
            m = jnp.max(a, axis=0, keepdims=True)
            e = jnp.exp2((a - m) * EXP2_SCALE)
            inv = 1.0 / jnp.sum(e, axis=0, keepdims=True)
            dp = dp_top[:, cols]
            center = jnp.sum(e * dp, axis=0, keepdims=True) * inv
            d_top[rows, cols] = (e * inv * (dp - center)).astype(BF16)
            a0 = s_top[rows, back]
            a1 = jnp.where(keep, s_low[rows, cols], -1e30)
            m = jnp.maximum(
                jnp.max(a0, axis=0, keepdims=True), jnp.max(a1, axis=0, keepdims=True)
            )
            e0 = jnp.exp2((a0 - m) * EXP2_SCALE)
            e1 = jnp.exp2((a1 - m) * EXP2_SCALE)
            inv = 1.0 / (jnp.sum(e0, axis=0, keepdims=True) + jnp.sum(e1, axis=0, keepdims=True))
            dp0 = dp_top[:, back]
            dp1 = dp_low[:, cols]
            center = (
                jnp.sum(e0 * dp0, axis=0, keepdims=True) + jnp.sum(e1 * dp1, axis=0, keepdims=True)
            ) * inv
            d_top[rows, back] = (e0 * inv * (dp0 - center)).astype(BF16)
            d_low[rows, cols] = (e1 * inv * (dp1 - center)).astype(BF16)


def step_kernel(
    nc, nt, donor_ref, heat_ref, w_ref, first_ref, second_ref, noise_ref, noise_b_ref,
    q_hbm, v_hbm, g_hbm, x_hbm,
    a_ref, b_ref,
    fa, fw, acc, base_ref, lr_ref, bt_ref,
    q_ref, v_ref, g_ref, x_ref, qt, qr, dp_top, dp_low, s_top, s_low, d_top, d_low,
    lgp, gbp, rc, gbc, part, sib, relay_in, near_in, far_in, ybuf, kept_a, kept_b, lg,
    ssem, rsem, esem, bsem, loadsem, csem, ksem, sibsem, relaysem, nearsem, ysem,
):
    at = Place(nc, nt)
    half, near, far = routes(at.nz)
    tokens = base_ref.shape[0]
    me = at.t
    rb = first_ref.shape[2]
    cb = second_ref.shape[1]
    hb = cb // 2
    npb = nt // nc
    nh = q_ref.shape[1] // HEAD
    early = nh * HEAD
    two = 2 * RANK
    lo, hi = slice(0, HEAD), slice(HEAD, tokens)
    across, sibling = (at.c, at.tok(1, 0)), (at.c, at.tok(0, 0, True))
    wide = pl.ds(pl.multiple_of(at.c * early, HEAD), early)
    narrow = pl.ds(pl.multiple_of(at.c * HEAD, HEAD), HEAD)
    loads = [
        pltpu.make_async_copy(q_hbm.at[:, wide], q_ref, loadsem.at[0]),
        pltpu.make_async_copy(v_hbm.at[:, narrow], v_ref, loadsem.at[1]),
        pltpu.make_async_copy(g_hbm.at[:, wide], g_ref, loadsem.at[2]),
        pltpu.make_async_copy(x_hbm, x_ref, loadsem.at[3]),
    ]
    for cp in loads:
        cp.start()

    fa[me, pl.ds(0, rb), :] = jnp.concatenate([first_ref[0], first_ref[1]], axis=0).T.astype(BF16)
    fa[me, pl.ds(rb, cb), :] = jnp.concatenate([second_ref[0], second_ref[1]], axis=1).astype(BF16)
    fw[me] = w_ref[...]
    close = [d for d in range(-near, near + 1) if d != 0]
    entry_barrier(
        [across, sibling]
        + [(at.c, at.tok(0, d)) for d in close]
        + [(at.chain(i), at.t) for i in range(1, nc)]
    )

    me_c = at.c

    def prepare():
        beside = []
        for j in range(2):
            heat = jnp.sqrt(jnp.full((1, rb), 2.0 * STRIDE_LENGTH * heat_ref[j], F32))
            kept_a[me_c, j * RANK : (j + 1) * RANK, :] = (
                (1.0 - STRIDE_LENGTH) * first_ref[j] + heat * noise_ref[j]
            ).astype(BF16)
            beside.append((1.0 - STRIDE_LENGTH) * second_ref[j] + heat[:, :RANK] * noise_b_ref[j])
        kept_b[me_c] = jnp.concatenate(beside, axis=1).astype(BF16)
        for h in range(nh):
            cols = slice(h * HEAD, (h + 1) * HEAD)
            later = slice(early + h * HEAD, early + (h + 1) * HEAD)
            q_t = q_ref[:, cols].astype(F32).T.astype(BF16)
            qt[:, cols] = q_t[:, lo]
            qt[:, later] = q_t[:, hi]
            qr[cols] = q_ref[lo, cols]
            qr[later] = q_ref[hi, cols]
            top = dot(v_ref[lo], g_ref[:, cols], ((1,), (1,)))
            dp_top[:, cols] = top[:, lo]
            dp_top[:, later] = top[:, hi]
            dp_low[:, cols] = dot(v_ref[hi], g_ref[hi, cols], ((1,), (1,)))

    swaps = []
    for i in range(1, nc):
        dev = (at.chain(i), at.t)
        swaps.append(remote(kept_a.at[me_c], kept_a.at[me_c], ksem.at[0, 0, i], ksem.at[0, 1, i], dev))
        swaps.append(remote(kept_b.at[me_c], kept_b.at[me_c], ksem.at[1, 0, i], ksem.at[1, 1, i], dev))

    full = (fa, fw)
    sends = []

    def send(kind, b, dev):
        cp = remote(full[kind].at[b], full[kind].at[b], ssem.at[len(sends)], rsem.at[kind, b], dev)
        cp.start()
        sends.append(cp)

    def wait(kind, b):
        remote(full[kind].at[b], full[kind].at[b], ssem.at[0], rsem.at[kind, b], sibling).wait_recv()

    def products(kind, blocks):
        total = acc[kind]
        for b in blocks:
            cols = pl.ds(pl.multiple_of(b * rb, rb), rb)
            total += dot(x_ref[:, cols], full[kind][b, pl.ds(0, rb), :])
        acc[kind] = total

    beside_me = [(at.c, at.tok(0, d)) for d in close]

    def levels(kind):
        first = []
        for d in sorted(close, key=abs):
            nxt = [across] if kind == 0 else []
            for f in far:
                if f * d < 0 and abs(d) == near:
                    nxt = [(at.c, at.tok(0, f + d))] + nxt
            first.append((0, d, nxt))
        first.append((1, 0, beside_me if kind == 1 else []))
        second = [(0, -f, [across]) for f in far] + [(1, d, []) for d in close]
        return [first, second, [(1, -f, []) for f in far]]

    groups = (levels(0), levels(1))

    def arrive(kind, group):
        blocks = []
        for other_yh, dz, nxt in group:
            b = at.tok(other_yh, dz)
            wait(kind, b)
            for dev in nxt:
                send(kind, b, dev)
            send(kind, b, sibling)
            blocks.append(b)
        return blocks

    def twins(kind, group):
        blocks = []
        for other_yh, dz, _ in group:
            b = at.tok(other_yh, dz, True)
            wait(kind, b)
            blocks.append(b)
        return blocks

    def b_copy(b):
        return remote(
            fa.at[b, pl.ds(rb, cb), :],
            bt_ref.at[at.c, lax.rem(b, npb)],
            bsem.at[0, b],
            bsem.at[1, at.c * npb + lax.rem(b, npb)],
            (b // npb, at.t),
        )

    def pass_on(blocks):
        for b in blocks:

            @pl.when(b // npb == at.c)
            def _():
                bt_ref[at.c, lax.rem(b, npb)] = fa[b, pl.ds(rb, cb), :]

            @pl.when(b // npb != at.c)
            def _():
                b_copy(b).start()

    own = [(0, 0, [])]
    for dev in beside_me + [across, sibling]:
        send(0, me, dev)
    acc[...] = jnp.zeros_like(acc)
    for cp in loads:
        cp.wait()
    prepare()
    here = arrive(0, groups[0][0])
    for dev in beside_me + [across, sibling]:
        send(1, me, dev)
    here += [me] + twins(0, own)
    pass_on(here)
    products(0, here)
    here = arrive(0, groups[0][1])
    there = arrive(1, groups[1][0])
    here += twins(0, groups[0][0])
    pass_on(here)
    products(0, here)
    here = arrive(0, groups[0][2]) + twins(0, groups[0][1]) + twins(0, groups[0][2])
    pass_on(here)
    products(0, here)

    exchanges = []
    lr_ref[at.c] = acc[0].astype(BF16)
    for i in range(1, nc):
        cp = remote(
            lr_ref.at[at.c], lr_ref.at[at.c], esem.at[0, i], esem.at[1, i], (at.chain(i), at.t)
        )
        cp.start()
        exchanges.append(cp)

    here = arrive(1, groups[1][1])
    products(1, there + here + [me] + twins(1, own) + twins(1, groups[1][0]))
    here = arrive(1, groups[1][2])
    products(1, here + twins(1, groups[1][1]) + twins(1, groups[1][2]))
    base_ref[...] = acc[1].astype(BF16)
    for cp in exchanges:
        cp.wait()
    for i in range(1, nc):
        for u in range(npb):
            remote(
                bt_ref.at[0, u],
                bt_ref.at[0, u],
                bsem.at[0, 0],
                bsem.at[1, at.chain(i) * npb + u],
                sibling,
            ).wait_recv()
    for cp in sends:
        cp.wait_send()

    for cp in swaps:
        cp.start()

    lane = lax.broadcasted_iota(jnp.int32, (HEAD, HEAD), 1)

    def heads_of(i):
        peer = at.chain(i)
        dev = (peer, at.t)
        return (
            remote(lgp.at[peer], rc.at[i], csem.at[0, 0, i], csem.at[0, 1, i], dev),
            remote(gbp.at[peer], gbc.at[at.c], csem.at[1, 0, i], csem.at[1, 1, i], dev),
        )

    def pair(p):
        keys, factors = [], []
        base = base_ref[...].astype(F32)
        for j in range(2):
            chain = donor_ref[2 * p + j]
            source = lax.shift_right_logical(chain, 1)
            odd = lax.bitwise_and(chain, 1)
            lr = lr_ref[source]
            bt = bt_ref[source].reshape(HEAD, HEAD).astype(F32)
            upper = (lane >= RANK).astype(jnp.int32)
            mine = jnp.where(upper == odd, bt, jnp.zeros_like(bt))
            keys.append((base + ADAPTER_SCALE * dot(lr, mine.astype(BF16), ((1,), (1,)))).astype(BF16))
            factors.append((odd == 1, lr, bt.T))
        s_top[...] = dot(jnp.concatenate([keys[0][lo], keys[1][lo]], axis=0), qt[...])
        s_low[...] = dot(jnp.concatenate([keys[0][hi], keys[1][hi]], axis=0), qt[:, early:])
        softmax_part(nh, s_top, s_low, dp_top, dp_low, d_top, d_low)
        grads_b = []
        kg_lo = (dot(d_top[...], qr[...]) * SCORE_SCALE).astype(BF16)
        kg_hi = (dot(d_low[...], qr[early:]) * SCORE_SCALE).astype(BF16)
        for j in range(2):
            odd, lr, b_rows = factors[j]
            here = slice(j * HEAD, (j + 1) * HEAD)
            kg = jnp.concatenate([kg_lo[here], kg_hi[here]], axis=0)
            b_mine = jnp.where(odd, b_rows[RANK:], b_rows[:RANK]).astype(BF16)
            lgp[p, j * RANK : (j + 1) * RANK, :] = (
                ADAPTER_SCALE * dot(b_mine, kg, ((1,), (1,)))
            ).astype(BF16)
            both = ADAPTER_SCALE * dot(kg, lr, ((0,), (0,)))
            grads_b.append(jnp.where(odd, both[:, RANK:], both[:, :RANK]))
        gbp[p] = jnp.concatenate(grads_b, axis=1).astype(BF16)

    def peer_pair(i, carry):
        pair(at.chain(i))

        @pl.when(i < nc)
        def _():
            for cp in heads_of(i):
                cp.start()

        return carry

    lax.fori_loop(1, nc + 1, peer_pair, 0)

    total = lgp[at.c].astype(F32)
    for i in range(1, nc):
        heads_of(i)[0].wait_recv()
        total += rc[i].astype(F32)
    lg[...] = total.astype(BF16)
    gbc[at.c] = gbp[at.c]
    for i in range(1, nc):
        heads_of(i)[1].wait_recv()

    far = sorted(far, key=lambda d: -abs(d))
    order = [(1, d) for d in far] + [(0, d) for d in far]
    order += [(1, d) for d in close] + [(0, d) for d in close] + [(1, 0), (0, 0)]

    def block(b):
        cols = pl.ds(pl.multiple_of(b * rb, rb), rb)
        start = pl.multiple_of(lax.rem(b, npb) * cb, cb)
        own_b = gbc.at[b // npb]
        second = jnp.concatenate(
            [own_b[pl.ds(start, hb), :], own_b[pl.ds(pl.multiple_of(start + hb, hb), hb), :]], axis=1
        )
        return dot(lg[...], x_ref[:, cols]), second

    sent = []
    passed = {}
    for i, (other_yh, dz) in enumerate(order):
        b = at.tok(other_yh, dz, True)
        first, second = block(b)
        part[b, pl.ds(0, two), :] = first.astype(BF16)
        part[b, pl.ds(two, hb), :] = second
        cp = remote(part.at[b], sib.at[i], sibsem.at[0, i], sibsem.at[1, i], sibling)
        cp.start()
        sent.append(cp)
        passed[other_yh, dz] = i, cp

    def join(other_yh, dz):
        i, cp = passed[other_yh, dz]
        b = at.tok(other_yh, dz)
        first, second = block(b)
        cp.wait_recv()
        part[b, pl.ds(0, two), :] = (first + sib[i, pl.ds(0, two), :].astype(F32)).astype(BF16)
        part[b, pl.ds(two, hb), :] = (
            second.astype(F32) + sib[i, pl.ds(two, hb), :].astype(F32)
        ).astype(BF16)
        return b

    def add(b, terms):
        value = part[b].astype(F32)
        for term in terms:
            value += term.astype(F32)
        return value

    def far_copy(dz):
        i = far.index(dz)
        return remote(part.at[at.tok(1, dz)], far_in.at[i], ysem.at[0, i], ysem.at[1, i], across)

    def relay(dz):
        i = far.index(dz)
        step = dz - near if dz > 0 else dz + near
        dev = (at.c, at.tok(0, step))
        return remote(part.at[at.tok(0, dz)], relay_in.at[i], relaysem.at[0, i], relaysem.at[1, i], dev)

    def direct(other_yh, dz):
        i = close.index(dz)
        return remote(
            part.at[at.tok(other_yh, dz)],
            near_in.at[other_yh, i],
            nearsem.at[0, other_yh, i],
            nearsem.at[1, other_yh, i],
            (at.c, at.tok(0, dz)),
        )

    def begin(cp):
        cp.start()
        sent.append(cp)
        return cp

    for dz in far:
        join(1, dz)
        begin(far_copy(dz))
    for dz in far:
        join(0, dz)
    for dz in close:
        join(1, dz)
    for dz in close:
        join(0, dz)
    join(1, 0)
    join(0, 0)
    for dz in far:
        b = at.tok(0, dz)
        far_copy(dz).wait_recv()
        part[b] = add(b, [far_in[far.index(dz)]]).astype(BF16)
        begin(relay(dz))
    for dz in close:
        begin(direct(1, dz))
        if abs(dz) < near:
            begin(direct(0, dz))
    for side in (1, -1):
        dz = side * near
        b = at.tok(0, dz)
        terms = []
        for d in far:
            if d * side > 0:
                relay(d).wait_recv()
                terms.append(relay_in[far.index(d)])
        part[b] = add(b, terms).astype(BF16)
        begin(direct(0, dz))

    def arrived(other_yh):
        for dz in close:
            direct(other_yh, dz).wait_recv()
        b = at.tok(other_yh, 0)
        return b, add(b, [near_in[other_yh, i] for i in range(len(close))])

    b, value = arrived(1)
    part[b] = value.astype(BF16)
    cross = remote(part.at[b], ybuf, ysem.at[0, len(far)], ysem.at[1, len(far)], across)
    cross.start()
    b, value = arrived(0)
    cross.wait()
    value += ybuf[...].astype(F32)
    sums_b = value[two:]

    for cp in swaps:
        cp.wait()
    for j in range(2):
        chain = donor_ref[2 * at.c + j]
        source = lax.shift_right_logical(chain, 1)
        odd = lax.bitwise_and(chain, 1) == 1
        whole = kept_a[source].astype(F32)
        rows = slice(j * RANK, (j + 1) * RANK)
        a_ref[j] = jnp.where(odd, whole[RANK:], whole[:RANK]) - STRIDE_LENGTH * value[rows]
        whole = kept_b[source].astype(F32)
        kept = jnp.where(odd, whole[:, RANK:], whole[:, :RANK])
        lanes = slice(j * RANK, (j + 1) * RANK)
        own_b = jnp.concatenate(
            [sums_b[:, lanes], sums_b[:, HEAD + j * RANK : HEAD + (j + 1) * RANK]], axis=0
        )
        b_ref[j] = kept - STRIDE_LENGTH * own_b
    for cp in sent:
        cp.wait_send()
    for i in range(1, nc):
        for cp in heads_of(i):
            cp.wait_send()

    def b_sent(b, carry):
        @pl.when(b // npb != at.c)
        def _():
            b_copy(b).wait_send()

        return carry

    lax.fori_loop(0, nt, b_sent, 0)


def step(nc, nt, donor, heats, w, first, second, noise, noise_b, q, v, g, x):
    tokens = x.shape[0]
    rb, cb = first.shape[2], second.shape[1]
    nz = nt // 4
    half, near, far = routes(nz)
    nh = q.shape[1] // (nc * HEAD)
    rows = 2 * RANK + cb // 2
    vmem = pl.BlockSpec(memory_space=pltpu.VMEM)
    smem = pl.BlockSpec(memory_space=pltpu.SMEM)
    hbm = pl.BlockSpec(memory_space=pl.ANY)
    sem = pltpu.SemaphoreType.DMA
    return pl.pallas_call(
        functools.partial(step_kernel, nc, nt),
        out_shape=(
            jax.ShapeDtypeStruct(first.shape, F32),
            jax.ShapeDtypeStruct(second.shape, F32),
        ),
        in_specs=[smem] * 2 + [vmem] * 5 + [hbm] * 4,
        out_specs=(vmem,) * 2,
        scratch_shapes=[
            pltpu.VMEM((nt, rb + cb, HEAD), BF16),
            pltpu.VMEM((nt, rb, HEAD), BF16),
            pltpu.VMEM((2, tokens, HEAD), F32),
            pltpu.VMEM((tokens, HEAD), BF16),
            pltpu.VMEM((nc, tokens, HEAD), BF16),
            pltpu.VMEM((nc, nt // nc, cb, HEAD), BF16),
            pltpu.VMEM((tokens, nh * HEAD), BF16),
            pltpu.VMEM((tokens, HEAD), BF16),
            pltpu.VMEM((tokens, nh * HEAD), BF16),
            pltpu.VMEM(x.shape, BF16),
            pltpu.VMEM((HEAD, nh * tokens), BF16),
            pltpu.VMEM((nh * tokens, HEAD), BF16),
            pltpu.VMEM((HEAD, nh * tokens), F32),
            pltpu.VMEM((HEAD, nh * HEAD), F32),
            pltpu.VMEM((2 * HEAD, nh * tokens), F32),
            pltpu.VMEM((2 * HEAD, nh * HEAD), F32),
            pltpu.VMEM((2 * HEAD, nh * tokens), BF16),
            pltpu.VMEM((2 * HEAD, nh * HEAD), BF16),
            pltpu.VMEM((nc, 2 * RANK, tokens), BF16),
            pltpu.VMEM((nc, HEAD, 2 * RANK), BF16),
            pltpu.VMEM((nc, 2 * RANK, tokens), BF16),
            pltpu.VMEM((nc, HEAD, 2 * RANK), BF16),
            pltpu.VMEM((nt, rows, rb), BF16),
            pltpu.VMEM((nt // 2, rows, rb), BF16),
            pltpu.VMEM((len(far), rows, rb), BF16),
            pltpu.VMEM((2, 2 * near, rows, rb), BF16),
            pltpu.VMEM((len(far), rows, rb), BF16),
            pltpu.VMEM((rows, rb), BF16),
            pltpu.VMEM((nc, 2 * RANK, rb), BF16),
            pltpu.VMEM((nc, cb, HEAD), BF16),
            pltpu.VMEM((2 * RANK, tokens), BF16),
            sem((4 * nt,)),
            sem((2, nt)),
            sem((2, nc)),
            sem((2, nt)),
            sem((4,)),
            sem((2, 2, nc)),
            sem((2, 2, nc)),
            sem((2, nt // 2)),
            sem((2, len(far))),
            sem((2, 2, 2 * near)),
            sem((2, len(far) + 1)),
        ],
        compiler_params=pltpu.CompilerParams(
            collective_id=0, has_side_effects=True, vmem_limit_bytes=VMEM_LIMIT
        ),
        name="step",
    )(donor, heats, w, first, second, noise, noise_b, q, v, g, x)


def settle_kernel(a_ref, b_ref, new_a_ref, new_b_ref):
    new_a_ref[...] = a_ref[...]
    new_b_ref[...] = b_ref[...]


def settle(a, b):
    vmem = pl.BlockSpec(memory_space=pltpu.VMEM)
    return pl.pallas_call(
        settle_kernel,
        out_shape=(jax.ShapeDtypeStruct(a.shape, F32), jax.ShapeDtypeStruct(b.shape, F32)),
        in_specs=[vmem] * 2,
        out_specs=(vmem,) * 2,
        name="settle",
    )(a, b)


def per_device(nc, nt, x, q, v, g, w, first, second, noise, noise_b, heats, donor):
    first, second, noise, noise_b = (z.transpose(0, 2, 1) for z in (first, second, noise, noise_b))
    new = settle(*step(nc, nt, donor, heats, w, first, second, noise, noise_b, q, v, g, x))
    return tuple(z.transpose(0, 2, 1) for z in new)


def solution(mesh):
    return jax.shard_map(
        functools.partial(per_device, mesh.shape["chain"], mesh.shape["tok"]),
        mesh=mesh,
        in_specs=(
            P("tok", None),
            P("tok", None),
            P("tok", None),
            P("tok", None),
            P("tok", "chain"),
            P("chain", "tok", None),
            P("chain", None, "tok"),
            P("chain", "tok", None),
            P("chain", None, "tok"),
            P("chain"),
            P(),
        ),
        out_specs=(P("chain", "tok", None), P("chain", None, "tok")),
        check_vma=False,
    )
```
